32 devices in a mesh: groups: 2 (over y), pix: 16 (over z, x, core).
Axes of the slice: x: 2, y: 2, z: 4, core: 2. Of those that a mesh axis runs over, the one named last changes fastest.
Arguments:
- new_obs: bfloat16 [24, 10, 32768], P(None, None, ('groups', 'pix')), parts along dimension 2, may hold values from -72 to 72
- old_obs: bfloat16 [24, 10, 32768], P(None, None, ('groups', 'pix')), parts along dimension 2, may hold values from -6 to 6
- new_mask: int32 [24, 32768], P(None, ('groups', 'pix')), parts along dimension 1, may hold values 0 or 1
- new_dates: int32 [24], replicated, may hold values from 0 to 1460
- old_dates: int32 [24], replicated, may hold values from 0 to 1460
- kept_gram: float32 [64, 32768], P(None, ('groups', 'pix')), parts along dimension 1, may hold values from -864 to 864, as said below
- kept_rhs: float32 [8, 10, 32768], P(None, None, ('groups', 'pix')), parts along dimension 2, may hold values from -6914 to 6914
Outputs:
- coefficients: float32 [8, 10, 32768], P(None, None, ('groups', 'pix')), parts along dimension 2
- retired: bfloat16 [24, 10, 32768], P(None, None, ('groups', 'pix')), parts along dimension 2
The draws below stay inside these ranges and needn't reach their ends.
There are 2 independent parts, one for each index of `groups`. The reference program is written for one: setup_inputs(seed, part) draws one part's arguments, and reference() takes and returns one part's arrays. A program takes and returns all parts, laid end to end along the dimension named above; an argument that names none is the same for every part. Nothing has to cross between parts.
Inputs may be any that keep to these rules, and one draw needn't show every extreme that they name: For every pixel, kept_gram holds the sums of products of design rows over the valid ones of 216 dates.
All inputs are finite; a program needn't handle non-finite values. No bound on the sum of `new_mask` on one device may be relied on, other than what follows from the above.
Results may differ from the reference program's by a relative error of at most 0.0004.
Values may be sent and summed in bfloat16 or wider, within the bound.
A program may use at most 64 MiB of HBM per device.

```python
import math
import jax
import jax.numpy as jnp
from jax import lax

B = 10
COEF = 8
NEW = 24
KEEP = 216
PIX_DEV = 1024
PIX = 16384
N_PIX = 16


OMEGA = 2.0 * math.pi / 365.25


CENTER = 730.0


YEAR_DAYS = 365.25


def harmonic_design(day_values):
    moment = day_values.astype(jnp.float32)
    columns = [jnp.ones_like(moment), (moment - CENTER) / YEAR_DAYS]
    for harmonic in range(1, 4):
        columns.append(jnp.cos(harmonic * OMEGA * moment))
        columns.append(jnp.sin(harmonic * OMEGA * moment))
    return jnp.stack(columns, axis=1)


def kept_sums(key):
    day_values = jax.random.randint(jax.random.fold_in(key, 11), (KEEP,), 0, 1461)
    valid = (jax.random.randint(jax.random.fold_in(key, 12), (KEEP, PIX), 0, 4) > 0).astype(jnp.float32)
    harmonic_rows = harmonic_design(day_values)
    paired = (harmonic_rows[:, :, None] * harmonic_rows[:, None, :]).reshape(KEEP, COEF * COEF)
    return jnp.dot(paired.T, valid, precision=lax.Precision.HIGHEST)


def draw_kept_gram(key, part):
    return kept_sums(key)


def draw_kept_rhs(key, part):
    gram_cube = kept_sums(key).reshape(COEF, COEF, PIX)
    base = jax.random.uniform(jax.random.fold_in(key, 13), (COEF, B, PIX), jnp.float32, -1.0, 1.0)
    noise = jax.random.uniform(jax.random.fold_in(key, 14), (COEF, B, PIX), jnp.float32, -2.0, 2.0)
    return jnp.einsum('acp,cbp->abp', gram_cube, base, precision=lax.Precision.HIGHEST) + noise


def draw_new_obs(key, part):
    position = jnp.arange(PIX).astype(jnp.float32) / PIX
    pixel_scale = jnp.exp(position * math.log(3.0) + jax.random.uniform(jax.random.fold_in(key, 21), (PIX,), jnp.float32, 0.0, math.log(3.0)))
    band_scale = jnp.exp(jax.random.uniform(jax.random.fold_in(key, 22), (B,), jnp.float32, math.log(0.5), math.log(2.0)))
    base = jax.random.truncated_normal(jax.random.fold_in(key, 23), -4.0, 4.0, (NEW, B, PIX), jnp.float32)
    values = base * band_scale[None, :, None] * pixel_scale[None, None, :]
    owners = PIX // PIX_DEV
    stride = PIX_DEV // owners
    shaped = values.reshape(NEW, B, owners, owners, stride)
    return shaped.transpose(0, 1, 3, 2, 4).reshape(NEW, B, PIX).astype(jnp.bfloat16)


def set_ends(array, stream_key, smallest, high):
    longest = array.shape.index(max(array.shape))
    spots = []
    for shift in (0, 1):
        where = [jax.random.randint(jax.random.fold_in(stream_key, axis), (), 0, length) for axis, length in enumerate(array.shape)]
        where[longest] = (where[longest] + shift) % array.shape[longest]
        spots.append(tuple(where))
    return array.at[spots[0]].set(smallest).at[spots[1]].set(high)


def block_scale(own_key, shape, cuts, least, largest):
    factor_of, own = 1.0, jax.random.fold_in(own_key, 6)
    for axis_at, shards_of in cuts:
        heights = jnp.exp(jax.random.uniform(jax.random.fold_in(own, axis_at), (shards_of,), jnp.float32, least / len(cuts), largest / len(cuts)))
        factor_of = factor_of * jnp.repeat(heights, shape[axis_at] // shards_of).reshape([-1 if axis == axis_at else 1 for axis in range(len(shape))])
    return factor_of


def normal_values(key, extent, scale, limit, pieces=(), kind=jnp.bfloat16):
    factor_of = block_scale(key, extent, pieces, -0.22, 0.18) if pieces else 1.0
    drawn = jax.random.normal(key, extent, jnp.float32) * scale * factor_of
    return jnp.minimum(jnp.maximum(drawn, -limit), limit).astype(kind)


def setup_inputs(seed: int = 0, part: int = 0) -> dict:
    keys = jax.random.split(jax.random.key(seed), 8)
    part_keys = jax.random.split(jax.random.fold_in(keys[7], part), 8)
    return {
        "new_obs": draw_new_obs(jax.random.fold_in(jax.random.fold_in(keys[7], part), 71), part),
        "old_obs": normal_values(part_keys[1], (NEW, B, PIX), 1.0, 6.0, ((2, 16),)),
        "new_mask": set_ends((jax.random.randint(part_keys[2], (NEW, PIX), 0, 4) < 3).astype(jnp.int32), jax.random.fold_in(part_keys[2], 1), 0, 1),
        "new_dates": set_ends(jax.random.randint(keys[3], (NEW,), 0, 1461), jax.random.fold_in(keys[3], 1), 0, 1460).astype(jnp.int32),
        "old_dates": set_ends(jax.random.randint(keys[4], (NEW,), 0, 1461), jax.random.fold_in(keys[4], 1), 0, 1460).astype(jnp.int32),
        "kept_gram": draw_kept_gram(jax.random.fold_in(jax.random.fold_in(keys[7], part), 71), part),
        "kept_rhs": draw_kept_rhs(jax.random.fold_in(jax.random.fold_in(keys[7], part), 71), part),
    }


OMEGA = 2.0 * math.pi / 365.25
CENTER = 730.0
YEAR_DAYS = 365.25
RIDGE = 0.5
EPSILON = 1e-06

def design(day_values):
    moment = day_values.astype(jnp.float32)
    columns = [jnp.ones_like(moment), (moment - CENTER) / YEAR_DAYS]
    for harmonic in range(1, 4):
        columns.append(jnp.cos(harmonic * OMEGA * moment))
        columns.append(jnp.sin(harmonic * OMEGA * moment))
    return jnp.stack(columns, axis=1)

def pair_rows(harmonic_rows):
    count = harmonic_rows.shape[0]
    terms = harmonic_rows.shape[1]
    return (harmonic_rows[:, :, None] * harmonic_rows[:, None, :]).reshape(count, terms * terms)

def cholesky_solve(normal_sums, right_sums):
    terms = right_sums.shape[0]
    factor = {}
    for row_at in range(terms):
        for col_at in range(row_at + 1):
            total = normal_sums[row_at * terms + col_at]
            if row_at == col_at:
                total = total + RIDGE
            for middle in range(col_at):
                total = total - factor[row_at, middle] * factor[col_at, middle]
            if row_at == col_at:
                factor[row_at, row_at] = jnp.sqrt(total)
            else:
                factor[row_at, col_at] = total / factor[col_at, col_at]
    forward = []
    for row_at in range(terms):
        total = right_sums[row_at]
        for middle in range(row_at):
            total = total - factor[row_at, middle][None, :] * forward[middle]
        forward.append(total / factor[row_at, row_at][None, :])
    backward = [None] * terms
    for row_at in reversed(range(terms)):
        total = forward[row_at]
        for middle in range(row_at + 1, terms):
            total = total - factor[middle, row_at][None, :] * backward[middle]
        backward[row_at] = total / factor[row_at, row_at][None, :]
    return jnp.stack(backward)

def corner(values):
    owners = N_PIX
    dates_count, band_count, total_pix = values.shape
    stride = total_pix // owners // owners
    shaped = values.reshape(dates_count, band_count, owners, owners, stride)
    return shaped.transpose(0, 1, 3, 2, 4).reshape(dates_count, band_count, total_pix)

def reference(new_obs, old_obs, new_mask, new_dates, old_dates, kept_gram, kept_rhs):
    highest = lax.Precision.HIGHEST
    entering = corner(new_obs)
    leaving = corner(old_obs)
    enter_rows = design(new_dates)
    leave_rows = design(old_dates)
    weights = new_mask.astype(jnp.float32)
    normal_sums = kept_gram + jnp.einsum('kn,kp->np', pair_rows(enter_rows), weights, precision=highest)
    observed = weights[:, None, :] * entering.astype(jnp.float32)
    right_sums = kept_rhs + jnp.einsum('ka,kbp->abp', enter_rows, observed, precision=highest)
    coefficients = cholesky_solve(normal_sums, right_sums)
    fitted = jnp.einsum('ka,abp->kbp', enter_rows, coefficients, precision=highest)
    misfit = weights[:, None, :] * (entering.astype(jnp.float32) - fitted)
    spread = lax.optimization_barrier(jnp.sum(misfit * misfit, axis=(0, 2))) / (NEW * PIX)
    inverse_spread = 1.0 / jnp.sqrt(spread + EPSILON)
    old_fit = jnp.einsum('ka,abp->kbp', leave_rows, coefficients, precision=highest)
    standard = ((leaving.astype(jnp.float32) - old_fit) * inverse_spread[None, :, None]).astype(jnp.bfloat16)
    return (coefficients, corner(standard))
```

```python
import functools
import math

import jax
import jax.numpy as jnp
from jax import lax
from jax.experimental import pallas as pl
from jax.experimental.pallas import tpu as pltpu
from jax.sharding import PartitionSpec as P

OMEGA = 2.0 * math.pi / 365.25
CENTER = 730.0
YEAR_DAYS = 365.25
RIDGE = 0.5
EPSILON = 1e-06
TERMS = 8
LANES = 128
MESH = pl.DeviceIdType.MESH


def design(day_values):
    moment = day_values.astype(jnp.float32)
    columns = [jnp.ones_like(moment), (moment - CENTER) / YEAR_DAYS]
    for harmonic in range(1, 4):
        columns.append(jnp.cos(harmonic * OMEGA * moment))
        columns.append(jnp.sin(harmonic * OMEGA * moment))
    return jnp.stack(columns, axis=1)


def pair_rows(harmonic_rows):
    count = harmonic_rows.shape[0]
    terms = harmonic_rows.shape[1]
    return (harmonic_rows[:, :, None] * harmonic_rows[:, None, :]).reshape(count, terms * terms)


def cholesky_solve(normal_sums, right_sums):
    terms = right_sums.shape[0]
    factor = {}
    for row_at in range(terms):
        for col_at in range(row_at + 1):
            total = normal_sums[row_at * terms + col_at]
            if row_at == col_at:
                total = total + RIDGE
            for middle in range(col_at):
                total = total - factor[row_at, middle] * factor[col_at, middle]
            if row_at == col_at:
                factor[row_at, row_at] = jnp.sqrt(total)
            else:
                factor[row_at, col_at] = total / factor[col_at, col_at]
    forward = []
    for row_at in range(terms):
        total = right_sums[row_at]
        for middle in range(row_at):
            total = total - factor[row_at, middle][None, :] * forward[middle]
        forward.append(total / factor[row_at, row_at][None, :])
    backward = [None] * terms
    for row_at in reversed(range(terms)):
        total = forward[row_at]
        for middle in range(row_at + 1, terms):
            total = total - factor[middle, row_at][None, :] * backward[middle]
        backward[row_at] = total / factor[row_at, row_at][None, :]
    return jnp.stack(backward)


def plain_on_device(new_obs, old_obs, new_mask, new_dates, old_dates, kept_gram, kept_rhs):
    highest = lax.Precision.HIGHEST
    owners = lax.axis_size("pix")
    dates_count, band_count, local_pix = new_obs.shape
    stride = local_pix // owners

    def split_owner(values):
        return values.reshape(values.shape[0], values.shape[1], owners, stride)

    def join_owner(values):
        return values.reshape(values.shape[0], values.shape[1], local_pix)

    entering = join_owner(
        lax.all_to_all(split_owner(new_obs), "pix", split_axis=2, concat_axis=2, tiled=True)
    )
    enter_rows = design(new_dates)
    leave_rows = design(old_dates)
    weights = new_mask.astype(jnp.float32)
    normal_sums = kept_gram + jnp.einsum(
        "kn,kp->np", pair_rows(enter_rows), weights, precision=highest
    )
    observed = weights[:, None, :] * entering.astype(jnp.float32)
    right_sums = kept_rhs + jnp.einsum("ka,kbp->abp", enter_rows, observed, precision=highest)
    coefficients = cholesky_solve(normal_sums, right_sums)
    fitted = jnp.einsum("ka,abp->kbp", enter_rows, coefficients, precision=highest)
    misfit = weights[:, None, :] * (entering.astype(jnp.float32) - fitted)
    spread = lax.psum(jnp.sum(misfit * misfit, axis=(0, 2)), "pix")
    inverse_spread = 1.0 / jnp.sqrt(spread / (dates_count * local_pix * owners) + EPSILON)
    tile_coefs = join_owner(
        lax.all_to_all(split_owner(coefficients), "pix", split_axis=2, concat_axis=2, tiled=True)
    )
    old_fit = jnp.einsum("ka,abp->kbp", leave_rows, tile_coefs, precision=highest)
    standard = ((old_obs.astype(jnp.float32) - old_fit) * inverse_spread[None, :, None]).astype(
        jnp.bfloat16
    )
    return (coefficients, standard)


def harmonic_values(moment, term):
    slope = (moment - CENTER) / YEAR_DAYS
    rate = jnp.where(
        term < 4,
        jnp.float32(1 * OMEGA),
        jnp.where(term < 6, jnp.float32(2 * OMEGA), jnp.float32(3 * OMEGA)),
    )
    angle = rate * moment
    wave = jnp.where(lax.rem(term, 2) == 0, jnp.cos(angle), jnp.sin(angle))
    return jnp.where(term == 0, 1.0, jnp.where(term == 1, slope, wave))


def narrow(values):
    return values.astype(jnp.bfloat16).astype(jnp.float32)


def three_parts(values):
    high = narrow(values)
    middle = narrow(values - high)
    return high, middle, values - high - middle


def days_along(dates_ref, count, shape, axis):
    at = lax.rem(lax.broadcasted_iota(jnp.int32, shape, axis), count)
    days = jnp.zeros(shape, jnp.int32)
    for date_at in range(count):
        days = jnp.where(at == date_at, dates_ref[date_at], days)
    return days.astype(jnp.float32)


def fit_table(dates_ref, dates_count, bands):
    width = bands * TERMS
    shape = (dates_count, 3 * width)
    days = days_along(dates_ref, dates_count, shape, 0)
    lane = lax.broadcasted_iota(jnp.int32, shape, 1)
    rows = harmonic_values(days, lax.rem(lane, TERMS))
    high = narrow(rows)
    rows = jnp.where(lane < 2 * width, high, rows - high)
    inner = lax.rem(lane, width)
    blocks = [
        jnp.where((inner >= band * TERMS) & (inner < (band + 1) * TERMS), rows, 0.0)
        for band in range(bands)
    ]
    return jnp.concatenate(blocks, axis=0).astype(jnp.bfloat16)


def stacked_parts(coefs):
    high = coefs.astype(jnp.bfloat16)
    low = (coefs - high.astype(jnp.float32)).astype(jnp.bfloat16)
    return jnp.concatenate([high, low, high], axis=0)


def pair_split(first, second, half):
    lane = lax.broadcasted_iota(jnp.int32, first.shape, 1)
    low = jnp.where(lane < half, first, pltpu.roll(second, half, 1))
    high = jnp.where(lane < half, pltpu.roll(first, half, 1), second)
    return low, high


def refit_kernel(
    owners,
    dates_count,
    bands,
    local_pix,
    x_hbm, old_hbm, mask_hbm, new_dates, old_dates, gram_hbm, rhs_hbm,
    coef_out, retired_out,
    x_ref, old_ref, mask_ref, gram_ref, rhs_ref,
    send_x, got_x, send_c, got_c, send_s, got_s,
    inverse_ref, right_table, enter_table, leave_table, square_ref, rest_ref,
    load_sem, x_send_sem, x_recv_sem, c_send_sem, c_recv_sem, s_send_sem, s_recv_sem,
):
    dot = lambda a, b: jnp.dot(a, b, preferred_element_type=jnp.float32)
    me = lax.axis_index("pix")
    half = LANES // 2
    tiles = local_pix // LANES
    rows = dates_count * bands
    width = TERMS * bands
    levels = owners.bit_length() - 1

    def flip(base, amount, bits):
        result = 0
        for level in range(bits):
            weight = 1 << level
            result = result + weight * ((base // weight + amount // weight) % 2)
        return result

    loads = [
        pltpu.make_async_copy(source, target, load_sem.at[at])
        for at, (source, target) in enumerate(
            ((x_hbm, x_ref), (mask_hbm, mask_ref), (gram_hbm, gram_ref), (rhs_hbm, rhs_ref), (old_hbm, old_ref))
        )
    ]
    for load in loads:
        load.start()
    barrier = pltpu.get_barrier_semaphore()
    for offset in range(1, owners):
        pl.semaphore_signal(
            barrier, inc=1, device_id={"pix": flip(me, offset, levels)}, device_id_type=MESH
        )

    loads[0].wait()
    for tile in range(tiles):
        values = x_ref[:, tile * LANES:(tile + 1) * LANES].astype(jnp.float32)
        low, high = pair_split(values[:rows // 2], values[rows // 2:], half)
        send_x[2 * tile] = low.astype(jnp.bfloat16)
        send_x[2 * tile + 1] = high.astype(jnp.bfloat16)
    pl.semaphore_wait(barrier, owners - 1)

    def remote(source, target, send_sem, recv_sem, peer):
        return pltpu.make_async_remote_copy(
            src_ref=source.at[peer],
            dst_ref=target.at[me],
            send_sem=send_sem.at[peer],
            recv_sem=recv_sem.at[me],
            device_id={"pix": peer},
            device_id_type=MESH,
        )

    def arrive(target, recv_sem, peer):
        pltpu.make_async_copy(target.at[peer], target.at[peer], recv_sem.at[peer]).wait()

    for offset in reversed(range(1, owners)):
        remote(send_x, got_x, x_send_sem, x_recv_sem, flip(me, offset, levels)).start()
    pltpu.make_async_copy(send_x.at[me], got_x.at[me], x_recv_sem.at[me]).start()

    lane = lax.broadcasted_iota(jnp.int32, (TERMS, rows), 1)
    across = harmonic_values(
        days_along(new_dates, dates_count, (TERMS, rows), 1),
        lax.broadcasted_iota(jnp.int32, (TERMS, rows), 0),
    )
    for part_at, part in enumerate(three_parts(across)):
        blocks = [
            jnp.where((lane >= band * dates_count) & (lane < (band + 1) * dates_count), part, 0.0)
            for band in range(bands)
        ]
        right_table[part_at * width:(part_at + 1) * width] = jnp.concatenate(blocks, axis=0).astype(jnp.bfloat16)
    enter_table[...] = fit_table(new_dates, dates_count, bands)
    leave_table[...] = fit_table(old_dates, dates_count, bands)

    design_rows = across[:, :dates_count]
    paired = jnp.concatenate([design_rows[at:at + 1] * design_rows for at in range(TERMS)], axis=0)
    loads[1].wait()
    loads[2].wait()
    weights = mask_ref[...].astype(jnp.float32).astype(jnp.bfloat16)
    normal = gram_ref[...]
    for part in reversed(three_parts(paired)):
        normal = normal + dot(part.astype(jnp.bfloat16), weights)
    sub = lax.broadcasted_iota(jnp.int32, (TERMS, local_pix), 0)
    matrix = [
        normal[at * TERMS:(at + 1) * TERMS] + jnp.where(sub == at, RIDGE, 0.0) for at in range(TERMS)
    ]
    for pivot in range(TERMS):
        scale = 1.0 / matrix[pivot][pivot:pivot + 1]
        pivot_row = jnp.where(sub == pivot, 1.0, matrix[pivot]) * scale
        for at in range(TERMS):
            if at != pivot:
                matrix[at] = (
                    jnp.where(sub == pivot, 0.0, matrix[at]) - matrix[at][pivot:pivot + 1] * pivot_row
                )
        matrix[pivot] = pivot_row
    for at in range(TERMS):
        inverse_ref[at] = matrix[at]

    square_ref[...] = jnp.zeros_like(square_ref)
    loads[3].wait()

    def own_step(step, carry):
        tile = flip(me // 2, step, levels - 1)
        columns = pl.ds(pl.multiple_of(tile * LANES, LANES), LANES)
        arrive(got_x, x_recv_sem, 2 * tile)
        arrive(got_x, x_recv_sem, 2 * tile + 1)
        low, high = pair_split(
            got_x[2 * tile].astype(jnp.float32), got_x[2 * tile + 1].astype(jnp.float32), half
        )
        entering = jnp.concatenate([low, high], axis=0)
        valid = mask_ref[:, columns].astype(jnp.float32)
        valid = jnp.concatenate([valid] * bands, axis=0)
        parts = dot(right_table[...], (entering * valid).astype(jnp.bfloat16))
        right = (parts[2 * width:] + parts[width:2 * width]) + parts[:width] + rhs_ref[:, columns]
        columns_of = [inverse_ref[at, :, columns] for at in range(TERMS)]
        solved = []
        for band in range(bands):
            total = None
            for at in range(TERMS):
                spot = band * TERMS + at
                term = columns_of[at] * right[spot:spot + 1]
                total = term if total is None else total + term
            solved.append(total)
        coefs = jnp.concatenate(solved, axis=0)
        coef_out[:, columns] = coefs
        low, high = pair_split(coefs[:width // 2], coefs[width // 2:], half)
        send_c[2 * tile] = low
        send_c[2 * tile + 1] = high
        fitted = dot(enter_table[...], stacked_parts(coefs))
        misfit = valid * (entering - fitted)
        square_ref[...] += misfit * misfit

        @pl.when(step > 0)
        def _():
            remote(send_c, got_c, c_send_sem, c_recv_sem, 2 * tile).start()
            remote(send_c, got_c, c_send_sem, c_recv_sem, 2 * tile + 1).start()

        @pl.when(step == 0)
        def _():
            remote(send_c, got_c, c_send_sem, c_recv_sem, flip(me, 1, levels)).start()
            pltpu.make_async_copy(send_c.at[me], got_c.at[me], c_recv_sem.at[me]).start()

        return carry

    lax.fori_loop(0, tiles, own_step, 0)

    spot = lax.broadcasted_iota(jnp.int32, (1, LANES), 1)
    local = jnp.zeros((1, LANES), jnp.float32)
    for band in range(bands):
        total = jnp.sum(square_ref[band * dates_count:(band + 1) * dates_count], axis=0, keepdims=True)
        local = jnp.where(spot == band, jnp.sum(total, axis=1, keepdims=True), local)
    send_s[...] = local

    def spread_copy(peer):
        return pltpu.make_async_remote_copy(
            src_ref=send_s,
            dst_ref=got_s.at[me],
            send_sem=s_send_sem.at[peer],
            recv_sem=s_recv_sem.at[me],
            device_id={"pix": peer},
            device_id_type=MESH,
        )

    for offset in reversed(range(1, owners)):
        spread_copy(flip(me, offset, levels)).start()
    pltpu.make_async_copy(send_s, got_s.at[me], s_recv_sem.at[me]).start()
    loads[4].wait()

    def rest_step(step, carry):
        tile = flip(me // 2, step, levels - 1)
        columns = pl.ds(pl.multiple_of(tile * LANES, LANES), LANES)
        arrive(got_c, c_recv_sem, 2 * tile)
        arrive(got_c, c_recv_sem, 2 * tile + 1)
        low, high = pair_split(got_c[2 * tile], got_c[2 * tile + 1], half)
        fitted = dot(leave_table[...], stacked_parts(jnp.concatenate([low, high], axis=0)))
        rest_ref[:, columns] = old_ref[:, columns].astype(jnp.float32) - fitted
        return carry

    lax.fori_loop(0, tiles, rest_step, 0)

    for peer in range(owners):
        arrive(got_s, s_recv_sem, peer)
    spread = jnp.sum(got_s[...], axis=0) / (dates_count * local_pix * owners)
    inverse_spread = 1.0 / jnp.sqrt(spread + EPSILON)
    for band in range(bands):
        scale = jnp.sum(jnp.where(spot == band, inverse_spread, 0.0), axis=1, keepdims=True)
        band_rows = slice(band * dates_count, (band + 1) * dates_count)
        rest_ref[band_rows] = rest_ref[band_rows] * scale
    retired_out[...] = rest_ref[...].astype(jnp.bfloat16)

    for offset in range(1, owners):
        peer = flip(me, offset, levels)
        remote(send_x, got_x, x_send_sem, x_recv_sem, peer).wait_send()
        remote(send_c, got_c, c_send_sem, c_recv_sem, peer).wait_send()
        spread_copy(peer).wait_send()


def fused_on_device(new_obs, old_obs, new_mask, new_dates, old_dates, kept_gram, kept_rhs):
    owners = lax.axis_size("pix")
    dates_count, bands, local_pix = new_obs.shape
    rows = dates_count * bands
    width = TERMS * bands
    band_major = lambda values: values.transpose(1, 0, 2).reshape(-1, local_pix)
    hbm = pl.BlockSpec(memory_space=pl.ANY)
    smem = pl.BlockSpec(memory_space=pltpu.SMEM)
    vmem = pl.BlockSpec(memory_space=pltpu.VMEM)
    f32, bf16 = jnp.float32, jnp.bfloat16
    dma = pltpu.SemaphoreType.DMA
    coefs, retired = pl.pallas_call(
        functools.partial(refit_kernel, owners, dates_count, bands, local_pix),
        out_shape=(
            jax.ShapeDtypeStruct((width, local_pix), f32),
            jax.ShapeDtypeStruct((rows, local_pix), bf16),
        ),
        in_specs=[hbm, hbm, hbm, smem, smem, hbm, hbm],
        out_specs=(vmem, vmem),
        scratch_shapes=[
            pltpu.VMEM((rows, local_pix), bf16),
            pltpu.VMEM((rows, local_pix), bf16),
            pltpu.VMEM((dates_count, local_pix), jnp.int32),
            pltpu.VMEM((TERMS * TERMS, local_pix), f32),
            pltpu.VMEM((width, local_pix), f32),
            pltpu.VMEM((owners, rows // 2, LANES), bf16),
            pltpu.VMEM((owners, rows // 2, LANES), bf16),
            pltpu.VMEM((owners, width // 2, LANES), f32),
            pltpu.VMEM((owners, width // 2, LANES), f32),
            pltpu.VMEM((1, LANES), f32),
            pltpu.VMEM((owners, 1, LANES), f32),
            pltpu.VMEM((TERMS, TERMS, local_pix), f32),
            pltpu.VMEM((3 * width, rows), bf16),
            pltpu.VMEM((rows, 3 * width), bf16),
            pltpu.VMEM((rows, 3 * width), bf16),
            pltpu.VMEM((rows, LANES), f32),
            pltpu.VMEM((rows, local_pix), f32),
            dma((5,)),
            dma((owners,)), dma((owners,)),
            dma((owners,)), dma((owners,)),
            dma((owners,)), dma((owners,)),
        ],
        compiler_params=pltpu.CompilerParams(collective_id=0, has_side_effects=True),
    )(
        band_major(new_obs), band_major(old_obs), new_mask, new_dates, old_dates, kept_gram,
        band_major(kept_rhs),
    )
    return (
        coefs.reshape(bands, TERMS, local_pix).transpose(1, 0, 2),
        retired.reshape(bands, dates_count, local_pix).transpose(1, 0, 2),
    )


def on_device(*arrays):
    owners = lax.axis_size("pix")
    dates_count, bands, local_pix = arrays[0].shape
    fits = (
        local_pix == owners * (LANES // 2)
        and owners & (owners - 1) == 0
        and arrays[6].shape[0] == TERMS
        and dates_count % 8 == 0
        and bands % 2 == 0
    )
    return fused_on_device(*arrays) if fits else plain_on_device(*arrays)


def solution(mesh):
    return jax.shard_map(
        on_device,
        mesh=mesh,
        in_specs=(
            P(None, None, ("groups", "pix")),
            P(None, None, ("groups", "pix")),
            P(None, ("groups", "pix")),
            P(),
            P(),
            P(None, ("groups", "pix")),
            P(None, None, ("groups", "pix")),
        ),
        out_specs=(P(None, None, ("groups", "pix")), P(None, None, ("groups", "pix"))),
        check_vma=False,
    )
```

```python
import functools
import math

import jax
import jax.numpy as jnp
from jax import lax
from jax.experimental import pallas as pl
from jax.experimental.pallas import tpu as pltpu
from jax.sharding import PartitionSpec as P

OMEGA = 2.0 * math.pi / 365.25
CENTER = 730.0
YEAR_DAYS = 365.25
RIDGE = 0.5
EPSILON = 1e-06
TERMS = 8
LANES = 128
MESH = pl.DeviceIdType.MESH


def design(day_values):
    moment = day_values.astype(jnp.float32)
    columns = [jnp.ones_like(moment), (moment - CENTER) / YEAR_DAYS]
    for harmonic in range(1, 4):
        columns.append(jnp.cos(harmonic * OMEGA * moment))
        columns.append(jnp.sin(harmonic * OMEGA * moment))
    return jnp.stack(columns, axis=1)


def pair_rows(harmonic_rows):
    count = harmonic_rows.shape[0]
    terms = harmonic_rows.shape[1]
    return (harmonic_rows[:, :, None] * harmonic_rows[:, None, :]).reshape(count, terms * terms)


def cholesky_solve(normal_sums, right_sums):
    terms = right_sums.shape[0]
    factor = {}
    for row_at in range(terms):
        for col_at in range(row_at + 1):
            total = normal_sums[row_at * terms + col_at]
            if row_at == col_at:
                total = total + RIDGE
            for middle in range(col_at):
                total = total - factor[row_at, middle] * factor[col_at, middle]
            if row_at == col_at:
                factor[row_at, row_at] = jnp.sqrt(total)
            else:
                factor[row_at, col_at] = total / factor[col_at, col_at]
    forward = []
    for row_at in range(terms):
        total = right_sums[row_at]
        for middle in range(row_at):
            total = total - factor[row_at, middle][None, :] * forward[middle]
        forward.append(total / factor[row_at, row_at][None, :])
    backward = [None] * terms
    for row_at in reversed(range(terms)):
        total = forward[row_at]
        for middle in range(row_at + 1, terms):
            total = total - factor[middle, row_at][None, :] * backward[middle]
        backward[row_at] = total / factor[row_at, row_at][None, :]
    return jnp.stack(backward)


def plain_on_device(new_obs, old_obs, new_mask, new_dates, old_dates, kept_gram, kept_rhs):
    highest = lax.Precision.HIGHEST
    owners = lax.axis_size("pix")
    dates_count, band_count, local_pix = new_obs.shape
    stride = local_pix // owners

    def split_owner(values):
        return values.reshape(values.shape[0], values.shape[1], owners, stride)

    def join_owner(values):
        return values.reshape(values.shape[0], values.shape[1], local_pix)

    entering = join_owner(
        lax.all_to_all(split_owner(new_obs), "pix", split_axis=2, concat_axis=2, tiled=True)
    )
    enter_rows = design(new_dates)
    leave_rows = design(old_dates)
    weights = new_mask.astype(jnp.float32)
    normal_sums = kept_gram + jnp.einsum(
        "kn,kp->np", pair_rows(enter_rows), weights, precision=highest
    )
    observed = weights[:, None, :] * entering.astype(jnp.float32)
    right_sums = kept_rhs + jnp.einsum("ka,kbp->abp", enter_rows, observed, precision=highest)
    coefficients = cholesky_solve(normal_sums, right_sums)
    fitted = jnp.einsum("ka,abp->kbp", enter_rows, coefficients, precision=highest)
    misfit = weights[:, None, :] * (entering.astype(jnp.float32) - fitted)
    spread = lax.psum(jnp.sum(misfit * misfit, axis=(0, 2)), "pix")
    inverse_spread = 1.0 / jnp.sqrt(spread / (dates_count * local_pix * owners) + EPSILON)
    tile_coefs = join_owner(
        lax.all_to_all(split_owner(coefficients), "pix", split_axis=2, concat_axis=2, tiled=True)
    )
    old_fit = jnp.einsum("ka,abp->kbp", leave_rows, tile_coefs, precision=highest)
    standard = ((old_obs.astype(jnp.float32) - old_fit) * inverse_spread[None, :, None]).astype(
        jnp.bfloat16
    )
    return (coefficients, standard)


def harmonic_values(moment, term):
    slope = (moment - CENTER) / YEAR_DAYS
    rate = jnp.where(
        term < 4,
        jnp.float32(1 * OMEGA),
        jnp.where(term < 6, jnp.float32(2 * OMEGA), jnp.float32(3 * OMEGA)),
    )
    angle = rate * moment
    wave = jnp.where(lax.rem(term, 2) == 0, jnp.cos(angle), jnp.sin(angle))
    return jnp.where(term == 0, 1.0, jnp.where(term == 1, slope, wave))


def narrow(values):
    return values.astype(jnp.bfloat16).astype(jnp.float32)


def three_parts(values):
    high = narrow(values)
    middle = narrow(values - high)
    return high, middle, values - high - middle


def days_along(dates_ref, count, shape, axis):
    at = lax.rem(lax.broadcasted_iota(jnp.int32, shape, axis), count)
    days = jnp.zeros(shape, jnp.int32)
    for date_at in range(count):
        days = jnp.where(at == date_at, dates_ref[date_at], days)
    return days.astype(jnp.float32)


def fit_table(dates_ref, dates_count, bands):
    width = bands * TERMS
    shape = (dates_count, 3 * width)
    days = days_along(dates_ref, dates_count, shape, 0)
    lane = lax.broadcasted_iota(jnp.int32, shape, 1)
    rows = harmonic_values(days, lax.rem(lane, TERMS))
    high = narrow(rows)
    rows = jnp.where(lane < 2 * width, high, rows - high)
    inner = lax.rem(lane, width)
    blocks = [
        jnp.where((inner >= band * TERMS) & (inner < (band + 1) * TERMS), rows, 0.0)
        for band in range(bands)
    ]
    return jnp.concatenate(blocks, axis=0).astype(jnp.bfloat16)


def stacked_parts(coefs):
    high = coefs.astype(jnp.bfloat16)
    low = (coefs - high.astype(jnp.float32)).astype(jnp.bfloat16)
    return jnp.concatenate([high, low, high], axis=0)


def pair_split(first, second, half):
    lane = lax.broadcasted_iota(jnp.int32, first.shape, 1)
    low = jnp.where(lane < half, first, pltpu.roll(second, half, 1))
    high = jnp.where(lane < half, pltpu.roll(first, half, 1), second)
    return low, high


def refit_kernel(
    owners,
    dates_count,
    bands,
    local_pix,
    x_hbm, old_hbm, mask_hbm, new_dates, old_dates, gram_hbm, rhs_hbm,
    coef_out, retired_out,
    x_ref, old_ref, mask_ref, gram_ref, rhs_ref,
    send_x, got_x, send_c, got_c, send_s, got_s,
    inverse_ref, right_table, enter_table, leave_table, square_ref, rest_ref,
    load_sem, x_send_sem, x_recv_sem, c_send_sem, c_recv_sem, s_send_sem, s_recv_sem,
):
    dot = lambda a, b: jnp.dot(a, b, preferred_element_type=jnp.float32)
    me = lax.axis_index("pix")
    half = LANES // 2
    tiles = local_pix // LANES
    rows = dates_count * bands
    width = TERMS * bands
    levels = owners.bit_length() - 1

    def flip(base, amount, bits):
        result = 0
        for level in range(bits):
            weight = 1 << level
            result = result + weight * ((base // weight + amount // weight) % 2)
        return result

    loads = [
        pltpu.make_async_copy(source, target, load_sem.at[at])
        for at, (source, target) in enumerate(
            ((x_hbm, x_ref), (mask_hbm, mask_ref), (gram_hbm, gram_ref), (rhs_hbm, rhs_ref), (old_hbm, old_ref))
        )
    ]
    for load in loads:
        load.start()
    barrier = pltpu.get_barrier_semaphore()
    for offset in range(1, owners):
        pl.semaphore_signal(
            barrier, inc=1, device_id={"pix": flip(me, offset, levels)}, device_id_type=MESH
        )

    loads[0].wait()
    for tile in range(tiles):
        values = x_ref[:, tile * LANES:(tile + 1) * LANES].astype(jnp.float32)
        low, high = pair_split(values[:rows // 2], values[rows // 2:], half)
        send_x[2 * tile] = low.astype(jnp.bfloat16)
        send_x[2 * tile + 1] = high.astype(jnp.bfloat16)
    pl.semaphore_wait(barrier, owners - 1)

    def remote(source, target, send_sem, recv_sem, peer):
        return pltpu.make_async_remote_copy(
            src_ref=source.at[peer],
            dst_ref=target.at[me],
            send_sem=send_sem.at[peer],
            recv_sem=recv_sem.at[me],
            device_id={"pix": peer},
            device_id_type=MESH,
        )

    def arrive(target, recv_sem, peer):
        pltpu.make_async_copy(target.at[peer], target.at[peer], recv_sem.at[peer]).wait()

    for offset in range(1, owners):
        remote(send_x, got_x, x_send_sem, x_recv_sem, flip(me, offset, levels)).start()
    pltpu.make_async_copy(send_x.at[me], got_x.at[me], x_recv_sem.at[me]).start()

    lane = lax.broadcasted_iota(jnp.int32, (TERMS, rows), 1)
    across = harmonic_values(
        days_along(new_dates, dates_count, (TERMS, rows), 1),
        lax.broadcasted_iota(jnp.int32, (TERMS, rows), 0),
    )
    for part_at, part in enumerate(three_parts(across)):
        blocks = [
            jnp.where((lane >= band * dates_count) & (lane < (band + 1) * dates_count), part, 0.0)
            for band in range(bands)
        ]
        right_table[part_at * width:(part_at + 1) * width] = jnp.concatenate(blocks, axis=0).astype(jnp.bfloat16)
    enter_table[...] = fit_table(new_dates, dates_count, bands)
    leave_table[...] = fit_table(old_dates, dates_count, bands)

    design_rows = across[:, :dates_count]
    paired = jnp.concatenate([design_rows[at:at + 1] * design_rows for at in range(TERMS)], axis=0)
    loads[1].wait()
    loads[2].wait()
    weights = mask_ref[...].astype(jnp.float32).astype(jnp.bfloat16)
    normal = gram_ref[...]
    for part in reversed(three_parts(paired)):
        normal = normal + dot(part.astype(jnp.bfloat16), weights)
    sub = lax.broadcasted_iota(jnp.int32, (TERMS, local_pix), 0)
    matrix = [
        normal[at * TERMS:(at + 1) * TERMS] + jnp.where(sub == at, RIDGE, 0.0) for at in range(TERMS)
    ]
    for pivot in range(TERMS):
        scale = 1.0 / matrix[pivot][pivot:pivot + 1]
        pivot_row = jnp.where(sub == pivot, 1.0, matrix[pivot]) * scale
        for at in range(TERMS):
            if at != pivot:
                matrix[at] = (
                    jnp.where(sub == pivot, 0.0, matrix[at]) - matrix[at][pivot:pivot + 1] * pivot_row
                )
        matrix[pivot] = pivot_row
    for at in range(TERMS):
        inverse_ref[at] = matrix[at]

    square_ref[...] = jnp.zeros_like(square_ref)
    loads[3].wait()

    def own_step(step, carry):
        tile = flip(me // 2, step, levels - 1)
        columns = pl.ds(pl.multiple_of(tile * LANES, LANES), LANES)
        arrive(got_x, x_recv_sem, 2 * tile)
        arrive(got_x, x_recv_sem, 2 * tile + 1)
        low, high = pair_split(
            got_x[2 * tile].astype(jnp.float32), got_x[2 * tile + 1].astype(jnp.float32), half
        )
        entering = jnp.concatenate([low, high], axis=0)
        valid = mask_ref[:, columns].astype(jnp.float32)
        valid = jnp.concatenate([valid] * bands, axis=0)
        parts = dot(right_table[...], (entering * valid).astype(jnp.bfloat16))
        right = (parts[2 * width:] + parts[width:2 * width]) + parts[:width] + rhs_ref[:, columns]
        columns_of = [inverse_ref[at, :, columns] for at in range(TERMS)]
        solved = []
        for band in range(bands):
            total = None
            for at in range(TERMS):
                spot = band * TERMS + at
                term = columns_of[at] * right[spot:spot + 1]
                total = term if total is None else total + term
            solved.append(total)
        coefs = jnp.concatenate(solved, axis=0)
        coef_out[:, columns] = coefs
        low, high = pair_split(coefs[:width // 2], coefs[width // 2:], half)
        send_c[2 * tile] = low
        send_c[2 * tile + 1] = high
        fitted = dot(enter_table[...], stacked_parts(coefs))
        misfit = valid * (entering - fitted)
        square_ref[...] += misfit * misfit

        @pl.when(step > 0)
        def _():
            remote(send_c, got_c, c_send_sem, c_recv_sem, 2 * tile).start()
            remote(send_c, got_c, c_send_sem, c_recv_sem, 2 * tile + 1).start()

        @pl.when(step == 0)
        def _():
            remote(send_c, got_c, c_send_sem, c_recv_sem, flip(me, 1, levels)).start()
            pltpu.make_async_copy(send_c.at[me], got_c.at[me], c_recv_sem.at[me]).start()

        return carry

    lax.fori_loop(0, tiles, own_step, 0)

    spot = lax.broadcasted_iota(jnp.int32, (1, LANES), 1)
    local = jnp.zeros((1, LANES), jnp.float32)
    for band in range(bands):
        total = jnp.sum(square_ref[band * dates_count:(band + 1) * dates_count], axis=0, keepdims=True)
        local = jnp.where(spot == band, jnp.sum(total, axis=1, keepdims=True), local)
    send_s[...] = local

    def spread_copy(peer):
        return pltpu.make_async_remote_copy(
            src_ref=send_s,
            dst_ref=got_s.at[me],
            send_sem=s_send_sem.at[peer],
            recv_sem=s_recv_sem.at[me],
            device_id={"pix": peer},
            device_id_type=MESH,
        )

    for offset in reversed(range(1, owners)):
        spread_copy(flip(me, offset, levels)).start()
    pltpu.make_async_copy(send_s, got_s.at[me], s_recv_sem.at[me]).start()
    loads[4].wait()

    def rest_step(step, carry):
        tile = flip(me // 2, step, levels - 1)
        columns = pl.ds(pl.multiple_of(tile * LANES, LANES), LANES)
        arrive(got_c, c_recv_sem, 2 * tile)
        arrive(got_c, c_recv_sem, 2 * tile + 1)
        low, high = pair_split(got_c[2 * tile], got_c[2 * tile + 1], half)
        fitted = dot(leave_table[...], stacked_parts(jnp.concatenate([low, high], axis=0)))
        rest_ref[:, columns] = old_ref[:, columns].astype(jnp.float32) - fitted
        return carry

    lax.fori_loop(0, tiles, rest_step, 0)

    for peer in range(owners):
        arrive(got_s, s_recv_sem, peer)
    spread = jnp.sum(got_s[...], axis=0) / (dates_count * local_pix * owners)
    inverse_spread = 1.0 / jnp.sqrt(spread + EPSILON)
    for band in range(bands):
        scale = jnp.sum(jnp.where(spot == band, inverse_spread, 0.0), axis=1, keepdims=True)
        band_rows = slice(band * dates_count, (band + 1) * dates_count)
        rest_ref[band_rows] = rest_ref[band_rows] * scale
    retired_out[...] = rest_ref[...].astype(jnp.bfloat16)

    for offset in range(1, owners):
        peer = flip(me, offset, levels)
        remote(send_x, got_x, x_send_sem, x_recv_sem, peer).wait_send()
        remote(send_c, got_c, c_send_sem, c_recv_sem, peer).wait_send()
        spread_copy(peer).wait_send()


def fused_on_device(new_obs, old_obs, new_mask, new_dates, old_dates, kept_gram, kept_rhs):
    owners = lax.axis_size("pix")
    dates_count, bands, local_pix = new_obs.shape
    rows = dates_count * bands
    width = TERMS * bands
    band_major = lambda values: values.transpose(1, 0, 2).reshape(-1, local_pix)
    hbm = pl.BlockSpec(memory_space=pltpu.HBM)
    smem = pl.BlockSpec(memory_space=pltpu.SMEM)
    vmem = pl.BlockSpec(memory_space=pltpu.VMEM)
    f32, bf16 = jnp.float32, jnp.bfloat16
    dma = pltpu.SemaphoreType.DMA
    coefs, retired = pl.pallas_call(
        functools.partial(refit_kernel, owners, dates_count, bands, local_pix),
        out_shape=(
            jax.ShapeDtypeStruct((width, local_pix), f32),
            jax.ShapeDtypeStruct((rows, local_pix), bf16),
        ),
        in_specs=[hbm, hbm, hbm, smem, smem, hbm, hbm],
        out_specs=(vmem, vmem),
        scratch_shapes=[
            pltpu.VMEM((rows, local_pix), bf16),
            pltpu.VMEM((rows, local_pix), bf16),
            pltpu.VMEM((dates_count, local_pix), jnp.int32),
            pltpu.VMEM((TERMS * TERMS, local_pix), f32),
            pltpu.VMEM((width, local_pix), f32),
            pltpu.VMEM((owners, rows // 2, LANES), bf16),
            pltpu.VMEM((owners, rows // 2, LANES), bf16),
            pltpu.VMEM((owners, width // 2, LANES), f32),
            pltpu.VMEM((owners, width // 2, LANES), f32),
            pltpu.VMEM((1, LANES), f32),
            pltpu.VMEM((owners, 1, LANES), f32),
            pltpu.VMEM((TERMS, TERMS, local_pix), f32),
            pltpu.VMEM((3 * width, rows), bf16),
            pltpu.VMEM((rows, 3 * width), bf16),
            pltpu.VMEM((rows, 3 * width), bf16),
            pltpu.VMEM((rows, LANES), f32),
            pltpu.VMEM((rows, local_pix), f32),
            dma((5,)),
            dma((owners,)), dma((owners,)),
            dma((owners,)), dma((owners,)),
            dma((owners,)), dma((owners,)),
        ],
        compiler_params=pltpu.CompilerParams(
            collective_id=0, has_side_effects=True, vmem_limit_bytes=20 << 20
        ),
    )(
        band_major(new_obs), band_major(old_obs), new_mask, new_dates, old_dates, kept_gram,
        band_major(kept_rhs),
    )
    return (
        coefs.reshape(bands, TERMS, local_pix).transpose(1, 0, 2),
        retired.reshape(bands, dates_count, local_pix).transpose(1, 0, 2),
    )


def on_device(*arrays):
    owners = lax.axis_size("pix")
    dates_count, bands, local_pix = arrays[0].shape
    fits = (
        local_pix == owners * (LANES // 2)
        and owners & (owners - 1) == 0
        and arrays[6].shape[0] == TERMS
        and dates_count % 8 == 0
        and bands % 2 == 0
    )
    return fused_on_device(*arrays) if fits else plain_on_device(*arrays)


def solution(mesh):
    return jax.shard_map(
        on_device,
        mesh=mesh,
        in_specs=(
            P(None, None, ("groups", "pix")),
            P(None, None, ("groups", "pix")),
            P(None, ("groups", "pix")),
            P(),
            P(),
            P(None, ("groups", "pix")),
            P(None, None, ("groups", "pix")),
        ),
        out_specs=(P(None, None, ("groups", "pix")), P(None, None, ("groups", "pix"))),
        check_vma=False,
    )
```

```python
import functools
import math

import jax
import jax.numpy as jnp
from jax import lax
from jax.experimental import pallas as pl
from jax.experimental.pallas import tpu as pltpu
from jax.sharding import PartitionSpec as P

OMEGA = 2.0 * math.pi / 365.25
CENTER = 730.0
YEAR_DAYS = 365.25
RIDGE = 0.5
EPSILON = 1e-06
TERMS = 8
LANES = 128
MESH = pl.DeviceIdType.MESH


def design(day_values):
    moment = day_values.astype(jnp.float32)
    columns = [jnp.ones_like(moment), (moment - CENTER) / YEAR_DAYS]
    for harmonic in range(1, 4):
        columns.append(jnp.cos(harmonic * OMEGA * moment))
        columns.append(jnp.sin(harmonic * OMEGA * moment))
    return jnp.stack(columns, axis=1)


def pair_rows(harmonic_rows):
    count = harmonic_rows.shape[0]
    terms = harmonic_rows.shape[1]
    return (harmonic_rows[:, :, None] * harmonic_rows[:, None, :]).reshape(count, terms * terms)


def cholesky_solve(normal_sums, right_sums):
    terms = right_sums.shape[0]
    factor = {}
    for row_at in range(terms):
        for col_at in range(row_at + 1):
            total = normal_sums[row_at * terms + col_at]
            if row_at == col_at:
                total = total + RIDGE
            for middle in range(col_at):
                total = total - factor[row_at, middle] * factor[col_at, middle]
            if row_at == col_at:
                factor[row_at, row_at] = jnp.sqrt(total)
            else:
                factor[row_at, col_at] = total / factor[col_at, col_at]
    forward = []
    for row_at in range(terms):
        total = right_sums[row_at]
        for middle in range(row_at):
            total = total - factor[row_at, middle][None, :] * forward[middle]
        forward.append(total / factor[row_at, row_at][None, :])
    backward = [None] * terms
    for row_at in reversed(range(terms)):
        total = forward[row_at]
        for middle in range(row_at + 1, terms):
            total = total - factor[middle, row_at][None, :] * backward[middle]
        backward[row_at] = total / factor[row_at, row_at][None, :]
    return jnp.stack(backward)


def plain_on_device(new_obs, old_obs, new_mask, new_dates, old_dates, kept_gram, kept_rhs):
    highest = lax.Precision.HIGHEST
    owners = lax.axis_size("pix")
    dates_count, band_count, local_pix = new_obs.shape
    stride = local_pix // owners

    def split_owner(values):
        return values.reshape(values.shape[0], values.shape[1], owners, stride)

    def join_owner(values):
        return values.reshape(values.shape[0], values.shape[1], local_pix)

    entering = join_owner(
        lax.all_to_all(split_owner(new_obs), "pix", split_axis=2, concat_axis=2, tiled=True)
    )
    enter_rows = design(new_dates)
    leave_rows = design(old_dates)
    weights = new_mask.astype(jnp.float32)
    normal_sums = kept_gram + jnp.einsum(
        "kn,kp->np", pair_rows(enter_rows), weights, precision=highest
    )
    observed = weights[:, None, :] * entering.astype(jnp.float32)
    right_sums = kept_rhs + jnp.einsum("ka,kbp->abp", enter_rows, observed, precision=highest)
    coefficients = cholesky_solve(normal_sums, right_sums)
    fitted = jnp.einsum("ka,abp->kbp", enter_rows, coefficients, precision=highest)
    misfit = weights[:, None, :] * (entering.astype(jnp.float32) - fitted)
    spread = lax.psum(jnp.sum(misfit * misfit, axis=(0, 2)), "pix")
    inverse_spread = 1.0 / jnp.sqrt(spread / (dates_count * local_pix * owners) + EPSILON)
    tile_coefs = join_owner(
        lax.all_to_all(split_owner(coefficients), "pix", split_axis=2, concat_axis=2, tiled=True)
    )
    old_fit = jnp.einsum("ka,abp->kbp", leave_rows, tile_coefs, precision=highest)
    standard = ((old_obs.astype(jnp.float32) - old_fit) * inverse_spread[None, :, None]).astype(
        jnp.bfloat16
    )
    return (coefficients, standard)


def harmonic_values(moment, term):
    slope = (moment - CENTER) / YEAR_DAYS
    rate = jnp.where(
        term < 4,
        jnp.float32(1 * OMEGA),
        jnp.where(term < 6, jnp.float32(2 * OMEGA), jnp.float32(3 * OMEGA)),
    )
    angle = rate * moment
    wave = jnp.where(lax.rem(term, 2) == 0, jnp.cos(angle), jnp.sin(angle))
    return jnp.where(term == 0, 1.0, jnp.where(term == 1, slope, wave))


def narrow(values):
    return values.astype(jnp.bfloat16).astype(jnp.float32)


def three_parts(values):
    high = narrow(values)
    middle = narrow(values - high)
    return high, middle, values - high - middle


def days_along(dates_ref, count, shape, axis):
    at = lax.rem(lax.broadcasted_iota(jnp.int32, shape, axis), count)
    days = jnp.zeros(shape, jnp.int32)
    for date_at in range(count):
        days = jnp.where(at == date_at, dates_ref[date_at], days)
    return days.astype(jnp.float32)


def fit_table(dates_ref, dates_count, bands):
    width = bands * TERMS
    shape = (dates_count, 3 * width)
    days = days_along(dates_ref, dates_count, shape, 0)
    lane = lax.broadcasted_iota(jnp.int32, shape, 1)
    rows = harmonic_values(days, lax.rem(lane, TERMS))
    high = narrow(rows)
    rows = jnp.where(lane < 2 * width, high, rows - high)
    inner = lax.rem(lane, width)
    blocks = [
        jnp.where((inner >= band * TERMS) & (inner < (band + 1) * TERMS), rows, 0.0)
        for band in range(bands)
    ]
    return jnp.concatenate(blocks, axis=0).astype(jnp.bfloat16)


def stacked_parts(coefs):
    high = coefs.astype(jnp.bfloat16)
    low = (coefs - high.astype(jnp.float32)).astype(jnp.bfloat16)
    return jnp.concatenate([high, low, high], axis=0)


def pair_split(first, second, half):
    lane = lax.broadcasted_iota(jnp.int32, first.shape, 1)
    low = jnp.where(lane < half, first, pltpu.roll(second, half, 1))
    high = jnp.where(lane < half, pltpu.roll(first, half, 1), second)
    return low, high


def refit_kernel(
    owners,
    dates_count,
    bands,
    local_pix,
    x_hbm, old_hbm, mask_hbm, new_dates_hbm, old_dates_hbm, gram_hbm, rhs_hbm,
    coef_out, retired_out,
    x_ref, old_ref, mask_ref, gram_ref, rhs_ref, new_dates, old_dates,
    send_x, got_x, send_c, got_c, send_s, got_s,
    inverse_ref, right_table, enter_table, leave_table, square_ref, rest_ref,
    load_sem, x_send_sem, x_recv_sem, c_send_sem, c_recv_sem, s_send_sem, s_recv_sem,
    relay_x, relay_c, x_relay_sem, x_pass_sem, c_relay_sem, c_pass_sem,
):
    dot = lambda a, b: jnp.dot(a, b, preferred_element_type=jnp.float32)
    me = lax.axis_index("pix")
    half = LANES // 2
    tiles = local_pix // LANES
    rows = dates_count * bands
    width = TERMS * bands
    levels = owners.bit_length() - 1

    def flip(base, amount, bits):
        result = 0
        for level in range(bits):
            weight = 1 << level
            result = result + weight * ((base // weight + amount // weight) % 2)
        return result

    loads = [
        pltpu.make_async_copy(source, target, load_sem.at[at])
        for at, (source, target) in enumerate(
            (
                (x_hbm, x_ref), (new_dates_hbm, new_dates), (old_dates_hbm, old_dates),
                (mask_hbm, mask_ref), (gram_hbm, gram_ref), (rhs_hbm, rhs_ref), (old_hbm, old_ref),
            )
        )
    ]
    for load in loads:
        load.start()
    barrier = pltpu.get_barrier_semaphore()
    for offset in range(1, owners):
        pl.semaphore_signal(
            barrier, inc=1, device_id={"pix": flip(me, offset, levels)}, device_id_type=MESH
        )

    loads[0].wait()
    for tile in range(tiles):
        values = x_ref[:, tile * LANES:(tile + 1) * LANES].astype(jnp.float32)
        low, high = pair_split(values[:rows // 2], values[rows // 2:], half)
        send_x[2 * tile] = low.astype(jnp.bfloat16)
        send_x[2 * tile + 1] = high.astype(jnp.bfloat16)
    pl.semaphore_wait(barrier, owners - 1)

    def remote(source, target, send_sem, recv_sem, peer):
        return pltpu.make_async_remote_copy(
            src_ref=source.at[peer],
            dst_ref=target.at[me],
            send_sem=send_sem.at[peer],
            recv_sem=recv_sem.at[me],
            device_id={"pix": peer},
            device_id_type=MESH,
        )

    def arrive(target, recv_sem, peer):
        pltpu.make_async_copy(target.at[peer], target.at[peer], recv_sem.at[peer]).wait()

    quarter = owners // 4
    behind = (me + owners - quarter) % owners
    ahead = (me + quarter) % owners
    c_relayed = range(owners // 2, owners // 2 + owners // 8)
    x_relayed = range(owners // 2 + owners // 8, owners // 2 + quarter)

    def first_leg(source, relay, send_sem, recv_sem, slot, peer):
        return pltpu.make_async_remote_copy(
            src_ref=source.at[peer],
            dst_ref=relay.at[slot],
            send_sem=send_sem.at[peer],
            recv_sem=recv_sem.at[slot],
            device_id={"pix": behind},
            device_id_type=MESH,
        )

    def second_leg(relay, target, send_sem, recv_sem, slot, offset):
        return pltpu.make_async_remote_copy(
            src_ref=relay.at[slot],
            dst_ref=target.at[ahead],
            send_sem=send_sem.at[slot],
            recv_sem=recv_sem.at[ahead],
            device_id={"pix": flip(ahead, offset, levels)},
            device_id_type=MESH,
        )

    for slot, offset in enumerate(x_relayed):
        first_leg(send_x, relay_x, x_send_sem, x_relay_sem, slot, flip(me, offset, levels)).start()
    for offset in range(1, owners):
        if offset not in x_relayed:
            remote(send_x, got_x, x_send_sem, x_recv_sem, flip(me, offset, levels)).start()
    pltpu.make_async_copy(send_x.at[me], got_x.at[me], x_recv_sem.at[me]).start()

    loads[1].wait()
    loads[2].wait()
    lane = lax.broadcasted_iota(jnp.int32, (TERMS, rows), 1)
    across = harmonic_values(
        days_along(new_dates, dates_count, (TERMS, rows), 1),
        lax.broadcasted_iota(jnp.int32, (TERMS, rows), 0),
    )
    for part_at, part in enumerate(three_parts(across)):
        blocks = [
            jnp.where((lane >= band * dates_count) & (lane < (band + 1) * dates_count), part, 0.0)
            for band in range(bands)
        ]
        right_table[part_at * width:(part_at + 1) * width] = jnp.concatenate(blocks, axis=0).astype(jnp.bfloat16)
    enter_table[...] = fit_table(new_dates, dates_count, bands)
    leave_table[...] = fit_table(old_dates, dates_count, bands)

    for slot, offset in enumerate(x_relayed):
        arrive(relay_x, x_relay_sem, slot)
        second_leg(relay_x, got_x, x_pass_sem, x_recv_sem, slot, offset).start()

    design_rows = across[:, :dates_count]
    paired = jnp.concatenate([design_rows[at:at + 1] * design_rows for at in range(TERMS)], axis=0)
    loads[3].wait()
    loads[4].wait()
    weights = mask_ref[...].astype(jnp.float32).astype(jnp.bfloat16)
    normal = gram_ref[...]
    for part in reversed(three_parts(paired)):
        normal = normal + dot(part.astype(jnp.bfloat16), weights)
    sub = lax.broadcasted_iota(jnp.int32, (TERMS, local_pix), 0)
    matrix = [
        normal[at * TERMS:(at + 1) * TERMS] + jnp.where(sub == at, RIDGE, 0.0) for at in range(TERMS)
    ]
    for pivot in range(TERMS):
        scale = 1.0 / matrix[pivot][pivot:pivot + 1]
        pivot_row = jnp.where(sub == pivot, 1.0, matrix[pivot]) * scale
        for at in range(TERMS):
            if at != pivot:
                matrix[at] = (
                    jnp.where(sub == pivot, 0.0, matrix[at]) - matrix[at][pivot:pivot + 1] * pivot_row
                )
        matrix[pivot] = pivot_row
    for at in range(TERMS):
        inverse_ref[at] = matrix[at]

    square_ref[...] = jnp.zeros_like(square_ref)
    loads[5].wait()

    def tile_at(step):
        far, near = step // quarter, step % quarter
        return flip(me // 2, quarter * far + (near + far * (quarter // 2)) % quarter, levels - 1)

    relayed_step = quarter + quarter // 2

    def own_step(step, carry):
        tile = tile_at(step)
        columns = pl.ds(pl.multiple_of(tile * LANES, LANES), LANES)
        arrive(got_x, x_recv_sem, 2 * tile)
        arrive(got_x, x_recv_sem, 2 * tile + 1)
        low, high = pair_split(
            got_x[2 * tile].astype(jnp.float32), got_x[2 * tile + 1].astype(jnp.float32), half
        )
        entering = jnp.concatenate([low, high], axis=0)
        valid = mask_ref[:, columns].astype(jnp.float32)
        valid = jnp.concatenate([valid] * bands, axis=0)
        parts = dot(right_table[...], (entering * valid).astype(jnp.bfloat16))
        right = (parts[2 * width:] + parts[width:2 * width]) + parts[:width] + rhs_ref[:, columns]
        columns_of = [inverse_ref[at, :, columns] for at in range(TERMS)]
        solved = []
        for band in range(bands):
            total = None
            for at in range(TERMS):
                spot = band * TERMS + at
                term = columns_of[at] * right[spot:spot + 1]
                total = term if total is None else total + term
            solved.append(total)
        coefs = jnp.concatenate(solved, axis=0)
        coef_out[:, columns] = coefs
        low, high = pair_split(coefs[:width // 2], coefs[width // 2:], half)
        send_c[2 * tile] = low
        send_c[2 * tile + 1] = high
        fitted = dot(enter_table[...], stacked_parts(coefs))
        misfit = valid * (entering - fitted)
        square_ref[...] += misfit * misfit

        relayed = (step >= relayed_step) & (step < relayed_step + len(c_relayed) // 2)

        @pl.when(relayed)
        def _():
            for part in range(2):
                slot = 2 * (step - relayed_step) + part
                peer = flip(me, owners // 2 + slot, levels)
                first_leg(send_c, relay_c, c_send_sem, c_relay_sem, slot, peer).start()

        @pl.when((step > 0) & jnp.logical_not(relayed))
        def _():
            remote(send_c, got_c, c_send_sem, c_recv_sem, 2 * tile).start()
            remote(send_c, got_c, c_send_sem, c_recv_sem, 2 * tile + 1).start()

        @pl.when(step == 0)
        def _():
            remote(send_c, got_c, c_send_sem, c_recv_sem, flip(me, 1, levels)).start()
            pltpu.make_async_copy(send_c.at[me], got_c.at[me], c_recv_sem.at[me]).start()

        return carry

    lax.fori_loop(0, tiles, own_step, 0)
    for slot, offset in enumerate(c_relayed):
        arrive(relay_c, c_relay_sem, slot)
        second_leg(relay_c, got_c, c_pass_sem, c_recv_sem, slot, offset).start()

    spot = lax.broadcasted_iota(jnp.int32, (1, LANES), 1)
    local = jnp.zeros((1, LANES), jnp.float32)
    for band in range(bands):
        total = jnp.sum(square_ref[band * dates_count:(band + 1) * dates_count], axis=0, keepdims=True)
        local = jnp.where(spot == band, jnp.sum(total, axis=1, keepdims=True), local)
    send_s[...] = local

    def spread_copy(peer):
        return pltpu.make_async_remote_copy(
            src_ref=send_s,
            dst_ref=got_s.at[me],
            send_sem=s_send_sem.at[peer],
            recv_sem=s_recv_sem.at[me],
            device_id={"pix": peer},
            device_id_type=MESH,
        )

    for offset in reversed(range(1, owners)):
        spread_copy(flip(me, offset, levels)).start()
    pltpu.make_async_copy(send_s, got_s.at[me], s_recv_sem.at[me]).start()
    loads[6].wait()

    def rest_step(step, carry):
        tile = tile_at(step)
        columns = pl.ds(pl.multiple_of(tile * LANES, LANES), LANES)
        arrive(got_c, c_recv_sem, 2 * tile)
        arrive(got_c, c_recv_sem, 2 * tile + 1)
        low, high = pair_split(got_c[2 * tile], got_c[2 * tile + 1], half)
        fitted = dot(leave_table[...], stacked_parts(jnp.concatenate([low, high], axis=0)))
        rest_ref[:, columns] = old_ref[:, columns].astype(jnp.float32) - fitted
        return carry

    lax.fori_loop(0, tiles, rest_step, 0)

    for peer in range(owners):
        arrive(got_s, s_recv_sem, peer)
    spread = jnp.sum(got_s[...], axis=0) / (dates_count * local_pix * owners)
    inverse_spread = 1.0 / jnp.sqrt(spread + EPSILON)
    for band in range(bands):
        scale = jnp.sum(jnp.where(spot == band, inverse_spread, 0.0), axis=1, keepdims=True)
        band_rows = slice(band * dates_count, (band + 1) * dates_count)
        rest_ref[band_rows] = rest_ref[band_rows] * scale
    retired_out[...] = rest_ref[...].astype(jnp.bfloat16)

    for offset in range(1, owners):
        peer = flip(me, offset, levels)
        remote(send_x, got_x, x_send_sem, x_recv_sem, peer).wait_send()
        remote(send_c, got_c, c_send_sem, c_recv_sem, peer).wait_send()
        spread_copy(peer).wait_send()
    for slot, offset in enumerate(x_relayed):
        second_leg(relay_x, got_x, x_pass_sem, x_recv_sem, slot, offset).wait_send()
    for slot, offset in enumerate(c_relayed):
        second_leg(relay_c, got_c, c_pass_sem, c_recv_sem, slot, offset).wait_send()


def fused_on_device(new_obs, old_obs, new_mask, new_dates, old_dates, kept_gram, kept_rhs):
    owners = lax.axis_size("pix")
    dates_count, bands, local_pix = new_obs.shape
    rows = dates_count * bands
    width = TERMS * bands
    stay = lambda values: pltpu.with_memory_space_constraint(values, pltpu.HBM)
    band_major = lambda values: stay(values.transpose(1, 0, 2).reshape(-1, local_pix))
    hbm = pl.BlockSpec(memory_space=pltpu.HBM)
    vmem = pl.BlockSpec(memory_space=pltpu.VMEM)
    f32, bf16 = jnp.float32, jnp.bfloat16
    dma = pltpu.SemaphoreType.DMA
    coefs, retired = pl.pallas_call(
        functools.partial(refit_kernel, owners, dates_count, bands, local_pix),
        out_shape=(
            jax.ShapeDtypeStruct((width, local_pix), f32),
            jax.ShapeDtypeStruct((rows, local_pix), bf16),
        ),
        in_specs=[hbm] * 7,
        out_specs=(vmem, vmem),
        scratch_shapes=[
            pltpu.VMEM((rows, local_pix), bf16),
            pltpu.VMEM((rows, local_pix), bf16),
            pltpu.VMEM((dates_count, local_pix), jnp.int32),
            pltpu.VMEM((TERMS * TERMS, local_pix), f32),
            pltpu.VMEM((width, local_pix), f32),
            pltpu.SMEM((dates_count,), jnp.int32),
            pltpu.SMEM((dates_count,), jnp.int32),
            pltpu.VMEM((owners, rows // 2, LANES), bf16),
            pltpu.VMEM((owners, rows // 2, LANES), bf16),
            pltpu.VMEM((owners, width // 2, LANES), f32),
            pltpu.VMEM((owners, width // 2, LANES), f32),
            pltpu.VMEM((1, LANES), f32),
            pltpu.VMEM((owners, 1, LANES), f32),
            pltpu.VMEM((TERMS, TERMS, local_pix), f32),
            pltpu.VMEM((3 * width, rows), bf16),
            pltpu.VMEM((rows, 3 * width), bf16),
            pltpu.VMEM((rows, 3 * width), bf16),
            pltpu.VMEM((rows, LANES), f32),
            pltpu.VMEM((rows, local_pix), f32),
            dma((7,)),
            dma((owners,)), dma((owners,)),
            dma((owners,)), dma((owners,)),
            dma((owners,)), dma((owners,)),
            pltpu.VMEM((owners // 8, rows // 2, LANES), bf16),
            pltpu.VMEM((owners // 8, width // 2, LANES), f32),
            dma((owners // 8,)), dma((owners // 8,)),
            dma((owners // 8,)), dma((owners // 8,)),
        ],
        compiler_params=pltpu.CompilerParams(
            collective_id=0, has_side_effects=True, vmem_limit_bytes=20 << 20
        ),
    )(
        band_major(new_obs), band_major(old_obs), stay(new_mask), stay(new_dates), stay(old_dates),
        stay(kept_gram), band_major(kept_rhs),
    )
    return (
        coefs.reshape(bands, TERMS, local_pix).transpose(1, 0, 2),
        retired.reshape(bands, dates_count, local_pix).transpose(1, 0, 2),
    )


def on_device(*arrays):
    owners = lax.axis_size("pix")
    dates_count, bands, local_pix = arrays[0].shape
    fits = (
        local_pix == owners * (LANES // 2)
        and owners >= 8
        and owners & (owners - 1) == 0
        and arrays[6].shape[0] == TERMS
        and dates_count % 8 == 0
        and bands % 2 == 0
    )
    return fused_on_device(*arrays) if fits else plain_on_device(*arrays)


def solution(mesh):
    return jax.shard_map(
        on_device,
        mesh=mesh,
        in_specs=(
            P(None, None, ("groups", "pix")),
            P(None, None, ("groups", "pix")),
            P(None, ("groups", "pix")),
            P(),
            P(),
            P(None, ("groups", "pix")),
            P(None, None, ("groups", "pix")),
        ),
        out_specs=(P(None, None, ("groups", "pix")), P(None, None, ("groups", "pix"))),
        check_vma=False,
    )
```

```python
import functools
import math

import jax
import jax.numpy as jnp
from jax import lax
from jax.experimental import pallas as pl
from jax.experimental.pallas import tpu as pltpu
from jax.sharding import PartitionSpec as P

OMEGA = 2.0 * math.pi / 365.25
CENTER = 730.0
YEAR_DAYS = 365.25
RIDGE = 0.5
EPSILON = 1e-06
TERMS = 8
LANES = 128
MESH = pl.DeviceIdType.MESH


def design(day_values):
    moment = day_values.astype(jnp.float32)
    columns = [jnp.ones_like(moment), (moment - CENTER) / YEAR_DAYS]
    for harmonic in range(1, 4):
        columns.append(jnp.cos(harmonic * OMEGA * moment))
        columns.append(jnp.sin(harmonic * OMEGA * moment))
    return jnp.stack(columns, axis=1)


def pair_rows(harmonic_rows):
    count = harmonic_rows.shape[0]
    terms = harmonic_rows.shape[1]
    return (harmonic_rows[:, :, None] * harmonic_rows[:, None, :]).reshape(count, terms * terms)


def cholesky_solve(normal_sums, right_sums):
    terms = right_sums.shape[0]
    factor = {}
    for row_at in range(terms):
        for col_at in range(row_at + 1):
            total = normal_sums[row_at * terms + col_at]
            if row_at == col_at:
                total = total + RIDGE
            for middle in range(col_at):
                total = total - factor[row_at, middle] * factor[col_at, middle]
            if row_at == col_at:
                factor[row_at, row_at] = jnp.sqrt(total)
            else:
                factor[row_at, col_at] = total / factor[col_at, col_at]
    forward = []
    for row_at in range(terms):
        total = right_sums[row_at]
        for middle in range(row_at):
            total = total - factor[row_at, middle][None, :] * forward[middle]
        forward.append(total / factor[row_at, row_at][None, :])
    backward = [None] * terms
    for row_at in reversed(range(terms)):
        total = forward[row_at]
        for middle in range(row_at + 1, terms):
            total = total - factor[middle, row_at][None, :] * backward[middle]
        backward[row_at] = total / factor[row_at, row_at][None, :]
    return jnp.stack(backward)


def plain_on_device(new_obs, old_obs, new_mask, new_dates, old_dates, kept_gram, kept_rhs):
    highest = lax.Precision.HIGHEST
    owners = lax.axis_size("pix")
    dates_count, band_count, local_pix = new_obs.shape
    stride = local_pix // owners

    def split_owner(values):
        return values.reshape(values.shape[0], values.shape[1], owners, stride)

    def join_owner(values):
        return values.reshape(values.shape[0], values.shape[1], local_pix)

    entering = join_owner(
        lax.all_to_all(split_owner(new_obs), "pix", split_axis=2, concat_axis=2, tiled=True)
    )
    enter_rows = design(new_dates)
    leave_rows = design(old_dates)
    weights = new_mask.astype(jnp.float32)
    normal_sums = kept_gram + jnp.einsum(
        "kn,kp->np", pair_rows(enter_rows), weights, precision=highest
    )
    observed = weights[:, None, :] * entering.astype(jnp.float32)
    right_sums = kept_rhs + jnp.einsum("ka,kbp->abp", enter_rows, observed, precision=highest)
    coefficients = cholesky_solve(normal_sums, right_sums)
    fitted = jnp.einsum("ka,abp->kbp", enter_rows, coefficients, precision=highest)
    misfit = weights[:, None, :] * (entering.astype(jnp.float32) - fitted)
    spread = lax.psum(jnp.sum(misfit * misfit, axis=(0, 2)), "pix")
    inverse_spread = 1.0 / jnp.sqrt(spread / (dates_count * local_pix * owners) + EPSILON)
    tile_coefs = join_owner(
        lax.all_to_all(split_owner(coefficients), "pix", split_axis=2, concat_axis=2, tiled=True)
    )
    old_fit = jnp.einsum("ka,abp->kbp", leave_rows, tile_coefs, precision=highest)
    standard = ((old_obs.astype(jnp.float32) - old_fit) * inverse_spread[None, :, None]).astype(
        jnp.bfloat16
    )
    return (coefficients, standard)


def harmonic_values(moment, term):
    slope = (moment - CENTER) / YEAR_DAYS
    rate = jnp.where(
        term < 4,
        jnp.float32(1 * OMEGA),
        jnp.where(term < 6, jnp.float32(2 * OMEGA), jnp.float32(3 * OMEGA)),
    )
    angle = rate * moment
    wave = jnp.where(lax.rem(term, 2) == 0, jnp.cos(angle), jnp.sin(angle))
    return jnp.where(term == 0, 1.0, jnp.where(term == 1, slope, wave))


def narrow(values):
    return values.astype(jnp.bfloat16).astype(jnp.float32)


def three_parts(values):
    high = narrow(values)
    middle = narrow(values - high)
    return high, middle, values - high - middle


def days_along(dates_ref, count, shape, axis):
    at = lax.rem(lax.broadcasted_iota(jnp.int32, shape, axis), count)
    days = jnp.zeros(shape, jnp.int32)
    for date_at in range(count):
        days = jnp.where(at == date_at, dates_ref[date_at], days)
    return days.astype(jnp.float32)


def fit_table(dates_ref, dates_count, bands):
    width = bands * TERMS
    shape = (dates_count, 3 * width)
    days = days_along(dates_ref, dates_count, shape, 0)
    lane = lax.broadcasted_iota(jnp.int32, shape, 1)
    rows = harmonic_values(days, lax.rem(lane, TERMS))
    high = narrow(rows)
    rows = jnp.where(lane < 2 * width, high, rows - high)
    inner = lax.rem(lane, width)
    blocks = [
        jnp.where((inner >= band * TERMS) & (inner < (band + 1) * TERMS), rows, 0.0)
        for band in range(bands)
    ]
    return jnp.concatenate(blocks, axis=0).astype(jnp.bfloat16)


def stacked_parts(coefs):
    high = coefs.astype(jnp.bfloat16)
    low = (coefs - high.astype(jnp.float32)).astype(jnp.bfloat16)
    return jnp.concatenate([high, low, high], axis=0)


def pair_split(first, second, half):
    lane = lax.broadcasted_iota(jnp.int32, first.shape, 1)
    low = jnp.where(lane < half, first, pltpu.roll(second, half, 1))
    high = jnp.where(lane < half, pltpu.roll(first, half, 1), second)
    return low, high


def refit_kernel(
    owners,
    dates_count,
    bands,
    local_pix,
    x_hbm, old_hbm, mask_hbm, new_dates_hbm, old_dates_hbm, gram_hbm, rhs_hbm,
    coef_out, retired_out,
    x_ref, old_ref, mask_ref, gram_ref, rhs_ref, new_dates, old_dates,
    send_x, got_x, send_c, got_c, send_s, got_s,
    inverse_ref, right_table, enter_table, leave_table, square_ref, rest_ref,
    load_sem, x_send_sem, x_recv_sem, c_send_sem, c_recv_sem, s_send_sem, s_recv_sem,
    relay_x, x_relay_sem, x_pass_sem,
):
    dot = lambda a, b: jnp.dot(a, b, preferred_element_type=jnp.float32)
    me = lax.axis_index("pix")
    half = LANES // 2
    tiles = local_pix // LANES
    rows = dates_count * bands
    width = TERMS * bands
    levels = owners.bit_length() - 1

    def flip(base, amount, bits):
        result = 0
        for level in range(bits):
            weight = 1 << level
            result = result + weight * ((base // weight + amount // weight) % 2)
        return result

    loads = [
        pltpu.make_async_copy(source, target, load_sem.at[at])
        for at, (source, target) in enumerate(
            (
                (x_hbm, x_ref), (new_dates_hbm, new_dates), (old_dates_hbm, old_dates),
                (mask_hbm, mask_ref), (gram_hbm, gram_ref), (rhs_hbm, rhs_ref), (old_hbm, old_ref),
            )
        )
    ]
    for load in loads:
        load.start()
    barrier = pltpu.get_barrier_semaphore()
    for offset in range(1, owners):
        pl.semaphore_signal(
            barrier, inc=1, device_id={"pix": flip(me, offset, levels)}, device_id_type=MESH
        )

    loads[0].wait()
    for tile in range(tiles):
        values = x_ref[:, tile * LANES:(tile + 1) * LANES].astype(jnp.float32)
        low, high = pair_split(values[:rows // 2], values[rows // 2:], half)
        send_x[2 * tile] = low.astype(jnp.bfloat16)
        send_x[2 * tile + 1] = high.astype(jnp.bfloat16)
    pl.semaphore_wait(barrier, owners - 1)

    def remote(source, target, send_sem, recv_sem, peer):
        return pltpu.make_async_remote_copy(
            src_ref=source.at[peer],
            dst_ref=target.at[me],
            send_sem=send_sem.at[peer],
            recv_sem=recv_sem.at[me],
            device_id={"pix": peer},
            device_id_type=MESH,
        )

    def arrive(target, recv_sem, peer):
        pltpu.make_async_copy(target.at[peer], target.at[peer], recv_sem.at[peer]).wait()

    quarter = owners // 4
    behind = (me + owners - quarter) % owners
    ahead = (me + quarter) % owners
    x_relayed = range(owners // 2 + owners // 8, owners // 2 + quarter)

    def first_leg(source, relay, send_sem, recv_sem, slot, peer):
        return pltpu.make_async_remote_copy(
            src_ref=source.at[peer],
            dst_ref=relay.at[slot],
            send_sem=send_sem.at[peer],
            recv_sem=recv_sem.at[slot],
            device_id={"pix": behind},
            device_id_type=MESH,
        )

    def second_leg(relay, target, send_sem, recv_sem, slot, offset):
        return pltpu.make_async_remote_copy(
            src_ref=relay.at[slot],
            dst_ref=target.at[ahead],
            send_sem=send_sem.at[slot],
            recv_sem=recv_sem.at[ahead],
            device_id={"pix": flip(ahead, offset, levels)},
            device_id_type=MESH,
        )

    for slot, offset in enumerate(x_relayed):
        first_leg(send_x, relay_x, x_send_sem, x_relay_sem, slot, flip(me, offset, levels)).start()
    for offset in range(1, owners):
        if offset not in x_relayed:
            remote(send_x, got_x, x_send_sem, x_recv_sem, flip(me, offset, levels)).start()
    pltpu.make_async_copy(send_x.at[me], got_x.at[me], x_recv_sem.at[me]).start()

    loads[1].wait()
    loads[2].wait()
    lane = lax.broadcasted_iota(jnp.int32, (TERMS, rows), 1)
    across = harmonic_values(
        days_along(new_dates, dates_count, (TERMS, rows), 1),
        lax.broadcasted_iota(jnp.int32, (TERMS, rows), 0),
    )
    for part_at, part in enumerate(three_parts(across)):
        blocks = [
            jnp.where((lane >= band * dates_count) & (lane < (band + 1) * dates_count), part, 0.0)
            for band in range(bands)
        ]
        right_table[part_at * width:(part_at + 1) * width] = jnp.concatenate(blocks, axis=0).astype(jnp.bfloat16)
    enter_table[...] = fit_table(new_dates, dates_count, bands)
    leave_table[...] = fit_table(old_dates, dates_count, bands)

    for slot, offset in enumerate(x_relayed):
        arrive(relay_x, x_relay_sem, slot)
        second_leg(relay_x, got_x, x_pass_sem, x_recv_sem, slot, offset).start()

    design_rows = across[:, :dates_count]
    paired = jnp.concatenate([design_rows[at:at + 1] * design_rows for at in range(TERMS)], axis=0)
    loads[3].wait()
    loads[4].wait()
    weights = mask_ref[...].astype(jnp.float32).astype(jnp.bfloat16)
    normal = gram_ref[...]
    for part in reversed(three_parts(paired)):
        normal = normal + dot(part.astype(jnp.bfloat16), weights)
    sub = lax.broadcasted_iota(jnp.int32, (TERMS, local_pix), 0)
    matrix = [
        normal[at * TERMS:(at + 1) * TERMS] + jnp.where(sub == at, RIDGE, 0.0) for at in range(TERMS)
    ]
    for pivot in range(TERMS):
        scale = 1.0 / matrix[pivot][pivot:pivot + 1]
        pivot_row = jnp.where(sub == pivot, 1.0, matrix[pivot]) * scale
        for at in range(TERMS):
            if at != pivot:
                matrix[at] = (
                    jnp.where(sub == pivot, 0.0, matrix[at]) - matrix[at][pivot:pivot + 1] * pivot_row
                )
        matrix[pivot] = pivot_row
    for at in range(TERMS):
        inverse_ref[at] = matrix[at]

    square_ref[...] = jnp.zeros_like(square_ref)
    loads[5].wait()

    def tile_at(step):
        far, near = step // quarter, step % quarter
        return flip(me // 2, quarter * far + (near + far * (quarter // 2)) % quarter, levels - 1)

    def own_step(step, carry):
        tile = tile_at(step)
        columns = pl.ds(pl.multiple_of(tile * LANES, LANES), LANES)
        arrive(got_x, x_recv_sem, 2 * tile)
        arrive(got_x, x_recv_sem, 2 * tile + 1)
        low, high = pair_split(
            got_x[2 * tile].astype(jnp.float32), got_x[2 * tile + 1].astype(jnp.float32), half
        )
        entering = jnp.concatenate([low, high], axis=0)
        valid = mask_ref[:, columns].astype(jnp.float32)
        valid = jnp.concatenate([valid] * bands, axis=0)
        parts = dot(right_table[...], (entering * valid).astype(jnp.bfloat16))
        right = (parts[2 * width:] + parts[width:2 * width]) + parts[:width] + rhs_ref[:, columns]
        columns_of = [inverse_ref[at, :, columns] for at in range(TERMS)]
        solved = []
        for band in range(bands):
            total = None
            for at in range(TERMS):
                spot = band * TERMS + at
                term = columns_of[at] * right[spot:spot + 1]
                total = term if total is None else total + term
            solved.append(total)
        coefs = jnp.concatenate(solved, axis=0)
        coef_out[:, columns] = coefs
        low, high = pair_split(coefs[:width // 2], coefs[width // 2:], half)
        send_c[2 * tile] = low
        send_c[2 * tile + 1] = high
        fitted = dot(enter_table[...], stacked_parts(coefs))
        misfit = valid * (entering - fitted)
        square_ref[...] += misfit * misfit

        @pl.when(step > 0)
        def _():
            remote(send_c, got_c, c_send_sem, c_recv_sem, 2 * tile).start()
            remote(send_c, got_c, c_send_sem, c_recv_sem, 2 * tile + 1).start()

        @pl.when(step == 0)
        def _():
            remote(send_c, got_c, c_send_sem, c_recv_sem, flip(me, 1, levels)).start()
            pltpu.make_async_copy(send_c.at[me], got_c.at[me], c_recv_sem.at[me]).start()

        return carry

    lax.fori_loop(0, tiles, own_step, 0)

    spot = lax.broadcasted_iota(jnp.int32, (1, LANES), 1)
    local = jnp.zeros((1, LANES), jnp.float32)
    for band in range(bands):
        total = jnp.sum(square_ref[band * dates_count:(band + 1) * dates_count], axis=0, keepdims=True)
        local = jnp.where(spot == band, jnp.sum(total, axis=1, keepdims=True), local)
    send_s[...] = local

    def spread_copy(peer):
        return pltpu.make_async_remote_copy(
            src_ref=send_s,
            dst_ref=got_s.at[me],
            send_sem=s_send_sem.at[peer],
            recv_sem=s_recv_sem.at[me],
            device_id={"pix": peer},
            device_id_type=MESH,
        )

    for offset in reversed(range(1, owners)):
        spread_copy(flip(me, offset, levels)).start()
    pltpu.make_async_copy(send_s, got_s.at[me], s_recv_sem.at[me]).start()
    loads[6].wait()

    def rest_step(step, carry):
        tile = tile_at(step)
        columns = pl.ds(pl.multiple_of(tile * LANES, LANES), LANES)
        arrive(got_c, c_recv_sem, 2 * tile)
        arrive(got_c, c_recv_sem, 2 * tile + 1)
        low, high = pair_split(got_c[2 * tile], got_c[2 * tile + 1], half)
        fitted = dot(leave_table[...], stacked_parts(jnp.concatenate([low, high], axis=0)))
        rest_ref[:, columns] = old_ref[:, columns].astype(jnp.float32) - fitted
        return carry

    lax.fori_loop(0, tiles, rest_step, 0)

    for peer in range(owners):
        arrive(got_s, s_recv_sem, peer)
    spread = jnp.sum(got_s[...], axis=0) / (dates_count * local_pix * owners)
    inverse_spread = 1.0 / jnp.sqrt(spread + EPSILON)
    for band in range(bands):
        scale = jnp.sum(jnp.where(spot == band, inverse_spread, 0.0), axis=1, keepdims=True)
        band_rows = slice(band * dates_count, (band + 1) * dates_count)
        rest_ref[band_rows] = rest_ref[band_rows] * scale
    retired_out[...] = rest_ref[...].astype(jnp.bfloat16)

    for offset in range(1, owners):
        peer = flip(me, offset, levels)
        remote(send_x, got_x, x_send_sem, x_recv_sem, peer).wait_send()
        remote(send_c, got_c, c_send_sem, c_recv_sem, peer).wait_send()
        spread_copy(peer).wait_send()
    for slot, offset in enumerate(x_relayed):
        second_leg(relay_x, got_x, x_pass_sem, x_recv_sem, slot, offset).wait_send()


def fused_on_device(new_obs, old_obs, new_mask, new_dates, old_dates, kept_gram, kept_rhs):
    owners = lax.axis_size("pix")
    dates_count, bands, local_pix = new_obs.shape
    rows = dates_count * bands
    width = TERMS * bands
    stay = lambda values: pltpu.with_memory_space_constraint(values, pltpu.HBM)
    band_major = lambda values: stay(values.transpose(1, 0, 2).reshape(-1, local_pix))
    hbm = pl.BlockSpec(memory_space=pltpu.HBM)
    vmem = pl.BlockSpec(memory_space=pltpu.VMEM)
    f32, bf16 = jnp.float32, jnp.bfloat16
    dma = pltpu.SemaphoreType.DMA
    coefs, retired = pl.pallas_call(
        functools.partial(refit_kernel, owners, dates_count, bands, local_pix),
        out_shape=(
            jax.ShapeDtypeStruct((width, local_pix), f32),
            jax.ShapeDtypeStruct((rows, local_pix), bf16),
        ),
        in_specs=[hbm] * 7,
        out_specs=(vmem, vmem),
        scratch_shapes=[
            pltpu.VMEM((rows, local_pix), bf16),
            pltpu.VMEM((rows, local_pix), bf16),
            pltpu.VMEM((dates_count, local_pix), jnp.int32),
            pltpu.VMEM((TERMS * TERMS, local_pix), f32),
            pltpu.VMEM((width, local_pix), f32),
            pltpu.SMEM((dates_count,), jnp.int32),
            pltpu.SMEM((dates_count,), jnp.int32),
            pltpu.VMEM((owners, rows // 2, LANES), bf16),
            pltpu.VMEM((owners, rows // 2, LANES), bf16),
            pltpu.VMEM((owners, width // 2, LANES), f32),
            pltpu.VMEM((owners, width // 2, LANES), f32),
            pltpu.VMEM((1, LANES), f32),
            pltpu.VMEM((owners, 1, LANES), f32),
            pltpu.VMEM((TERMS, TERMS, local_pix), f32),
            pltpu.VMEM((3 * width, rows), bf16),
            pltpu.VMEM((rows, 3 * width), bf16),
            pltpu.VMEM((rows, 3 * width), bf16),
            pltpu.VMEM((rows, LANES), f32),
            pltpu.VMEM((rows, local_pix), f32),
            dma((7,)),
            dma((owners,)), dma((owners,)),
            dma((owners,)), dma((owners,)),
            dma((owners,)), dma((owners,)),
            pltpu.VMEM((owners // 8, rows // 2, LANES), bf16),
            dma((owners // 8,)), dma((owners // 8,)),
        ],
        compiler_params=pltpu.CompilerParams(
            collective_id=0, has_side_effects=True, vmem_limit_bytes=20 << 20
        ),
    )(
        band_major(new_obs), band_major(old_obs), stay(new_mask), stay(new_dates), stay(old_dates),
        stay(kept_gram), band_major(kept_rhs),
    )
    return (
        coefs.reshape(bands, TERMS, local_pix).transpose(1, 0, 2),
        retired.reshape(bands, dates_count, local_pix).transpose(1, 0, 2),
    )


def on_device(*arrays):
    owners = lax.axis_size("pix")
    dates_count, bands, local_pix = arrays[0].shape
    fits = (
        local_pix == owners * (LANES // 2)
        and owners >= 8
        and owners & (owners - 1) == 0
        and arrays[6].shape[0] == TERMS
        and dates_count % 8 == 0
        and bands % 2 == 0
    )
    return fused_on_device(*arrays) if fits else plain_on_device(*arrays)


def solution(mesh):
    return jax.shard_map(
        on_device,
        mesh=mesh,
        in_specs=(
            P(None, None, ("groups", "pix")),
            P(None, None, ("groups", "pix")),
            P(None, ("groups", "pix")),
            P(),
            P(),
            P(None, ("groups", "pix")),
            P(None, None, ("groups", "pix")),
        ),
        out_specs=(P(None, None, ("groups", "pix")), P(None, None, ("groups", "pix"))),
        check_vma=False,
    )
```

```python
import functools
import math

import jax
import jax.numpy as jnp
from jax import lax
from jax.experimental import pallas as pl
from jax.experimental.pallas import tpu as pltpu
from jax.sharding import PartitionSpec as P

OMEGA = 2.0 * math.pi / 365.25
CENTER = 730.0
YEAR_DAYS = 365.25
RIDGE = 0.5
EPSILON = 1e-06
TERMS = 8
LANES = 128
MESH = pl.DeviceIdType.MESH


def design(day_values):
    moment = day_values.astype(jnp.float32)
    columns = [jnp.ones_like(moment), (moment - CENTER) / YEAR_DAYS]
    for harmonic in range(1, 4):
        columns.append(jnp.cos(harmonic * OMEGA * moment))
        columns.append(jnp.sin(harmonic * OMEGA * moment))
    return jnp.stack(columns, axis=1)


def pair_rows(harmonic_rows):
    count = harmonic_rows.shape[0]
    terms = harmonic_rows.shape[1]
    return (harmonic_rows[:, :, None] * harmonic_rows[:, None, :]).reshape(count, terms * terms)


def cholesky_solve(normal_sums, right_sums):
    terms = right_sums.shape[0]
    factor = {}
    for row_at in range(terms):
        for col_at in range(row_at + 1):
            total = normal_sums[row_at * terms + col_at]
            if row_at == col_at:
                total = total + RIDGE
            for middle in range(col_at):
                total = total - factor[row_at, middle] * factor[col_at, middle]
            if row_at == col_at:
                factor[row_at, row_at] = jnp.sqrt(total)
            else:
                factor[row_at, col_at] = total / factor[col_at, col_at]
    forward = []
    for row_at in range(terms):
        total = right_sums[row_at]
        for middle in range(row_at):
            total = total - factor[row_at, middle][None, :] * forward[middle]
        forward.append(total / factor[row_at, row_at][None, :])
    backward = [None] * terms
    for row_at in reversed(range(terms)):
        total = forward[row_at]
        for middle in range(row_at + 1, terms):
            total = total - factor[middle, row_at][None, :] * backward[middle]
        backward[row_at] = total / factor[row_at, row_at][None, :]
    return jnp.stack(backward)


def plain_on_device(new_obs, old_obs, new_mask, new_dates, old_dates, kept_gram, kept_rhs):
    highest = lax.Precision.HIGHEST
    owners = lax.axis_size("pix")
    dates_count, band_count, local_pix = new_obs.shape
    stride = local_pix // owners

    def split_owner(values):
        return values.reshape(values.shape[0], values.shape[1], owners, stride)

    def join_owner(values):
        return values.reshape(values.shape[0], values.shape[1], local_pix)

    entering = join_owner(
        lax.all_to_all(split_owner(new_obs), "pix", split_axis=2, concat_axis=2, tiled=True)
    )
    enter_rows = design(new_dates)
    leave_rows = design(old_dates)
    weights = new_mask.astype(jnp.float32)
    normal_sums = kept_gram + jnp.einsum(
        "kn,kp->np", pair_rows(enter_rows), weights, precision=highest
    )
    observed = weights[:, None, :] * entering.astype(jnp.float32)
    right_sums = kept_rhs + jnp.einsum("ka,kbp->abp", enter_rows, observed, precision=highest)
    coefficients = cholesky_solve(normal_sums, right_sums)
    fitted = jnp.einsum("ka,abp->kbp", enter_rows, coefficients, precision=highest)
    misfit = weights[:, None, :] * (entering.astype(jnp.float32) - fitted)
    spread = lax.psum(jnp.sum(misfit * misfit, axis=(0, 2)), "pix")
    inverse_spread = 1.0 / jnp.sqrt(spread / (dates_count * local_pix * owners) + EPSILON)
    tile_coefs = join_owner(
        lax.all_to_all(split_owner(coefficients), "pix", split_axis=2, concat_axis=2, tiled=True)
    )
    old_fit = jnp.einsum("ka,abp->kbp", leave_rows, tile_coefs, precision=highest)
    standard = ((old_obs.astype(jnp.float32) - old_fit) * inverse_spread[None, :, None]).astype(
        jnp.bfloat16
    )
    return (coefficients, standard)


def harmonic_values(moment, term):
    slope = (moment - CENTER) / YEAR_DAYS
    rate = jnp.where(
        term < 4,
        jnp.float32(1 * OMEGA),
        jnp.where(term < 6, jnp.float32(2 * OMEGA), jnp.float32(3 * OMEGA)),
    )
    angle = rate * moment
    wave = jnp.where(lax.rem(term, 2) == 0, jnp.cos(angle), jnp.sin(angle))
    return jnp.where(term == 0, 1.0, jnp.where(term == 1, slope, wave))


def narrow(values):
    return values.astype(jnp.bfloat16).astype(jnp.float32)


def three_parts(values):
    high = narrow(values)
    middle = narrow(values - high)
    return high, middle, values - high - middle


def days_along(dates_ref, count, shape, axis):
    at = lax.rem(lax.broadcasted_iota(jnp.int32, shape, axis), count)
    days = jnp.zeros(shape, jnp.int32)
    for date_at in range(count):
        days = jnp.where(at == date_at, dates_ref[date_at], days)
    return days.astype(jnp.float32)


def fit_table(dates_ref, dates_count, bands):
    width = bands * TERMS
    shape = (dates_count, 3 * width)
    days = days_along(dates_ref, dates_count, shape, 0)
    lane = lax.broadcasted_iota(jnp.int32, shape, 1)
    rows = harmonic_values(days, lax.rem(lane, TERMS))
    high = narrow(rows)
    rows = jnp.where(lane < 2 * width, high, rows - high)
    inner = lax.rem(lane, width)
    blocks = [
        jnp.where((inner >= band * TERMS) & (inner < (band + 1) * TERMS), rows, 0.0)
        for band in range(bands)
    ]
    return jnp.concatenate(blocks, axis=0).astype(jnp.bfloat16)


def stacked_parts(coefs):
    high = coefs.astype(jnp.bfloat16)
    low = (coefs - high.astype(jnp.float32)).astype(jnp.bfloat16)
    return jnp.concatenate([high, low, high], axis=0)


def pair_split(first, second, half):
    lane = lax.broadcasted_iota(jnp.int32, first.shape, 1)
    low = jnp.where(lane < half, first, pltpu.roll(second, half, 1))
    high = jnp.where(lane < half, pltpu.roll(first, half, 1), second)
    return low, high


def refit_kernel(
    owners,
    dates_count,
    bands,
    local_pix,
    x_hbm, old_hbm, mask_hbm, new_dates_hbm, old_dates_hbm, gram_hbm, rhs_hbm,
    coef_out, retired_out,
    x_ref, old_ref, mask_ref, gram_ref, rhs_ref, new_dates, old_dates,
    send_x, got_x, send_c, got_c, send_s, got_s,
    inverse_ref, right_table, enter_table, leave_table, square_ref, rest_ref,
    load_sem, x_send_sem, x_recv_sem, c_send_sem, c_recv_sem, s_send_sem, s_recv_sem,
    relay_x, x_relay_sem, x_pass_sem,
):
    dot = lambda a, b: jnp.dot(a, b, preferred_element_type=jnp.float32)
    me = lax.axis_index("pix")
    half = LANES // 2
    tiles = local_pix // LANES
    rows = dates_count * bands
    width = TERMS * bands
    levels = owners.bit_length() - 1

    def flip(base, amount, bits):
        result = 0
        for level in range(bits):
            weight = 1 << level
            result = result + weight * ((base // weight + amount // weight) % 2)
        return result

    loads = [
        pltpu.make_async_copy(source, target, load_sem.at[at])
        for at, (source, target) in enumerate(
            (
                (x_hbm, x_ref), (new_dates_hbm, new_dates), (old_dates_hbm, old_dates),
                (mask_hbm, mask_ref), (gram_hbm, gram_ref), (rhs_hbm, rhs_ref), (old_hbm, old_ref),
            )
        )
    ]
    for load in loads:
        load.start()
    barrier = pltpu.get_barrier_semaphore()
    for offset in range(1, owners):
        pl.semaphore_signal(
            barrier, inc=1, device_id={"pix": flip(me, offset, levels)}, device_id_type=MESH
        )

    loads[0].wait()
    for tile in range(tiles):
        values = x_ref[:, tile * LANES:(tile + 1) * LANES].astype(jnp.float32)
        low, high = pair_split(values[:rows // 2], values[rows // 2:], half)
        send_x[2 * tile] = low.astype(jnp.bfloat16)
        send_x[2 * tile + 1] = high.astype(jnp.bfloat16)
    pl.semaphore_wait(barrier, owners - 1)

    def remote(source, target, send_sem, recv_sem, peer):
        return pltpu.make_async_remote_copy(
            src_ref=source.at[peer],
            dst_ref=target.at[me],
            send_sem=send_sem.at[peer],
            recv_sem=recv_sem.at[me],
            device_id={"pix": peer},
            device_id_type=MESH,
        )

    def arrive(target, recv_sem, peer):
        pltpu.make_async_copy(target.at[peer], target.at[peer], recv_sem.at[peer]).wait()

    quarter = owners // 4
    behind = (me + owners - quarter) % owners
    ahead = (me + quarter) % owners
    x_relayed = range(owners // 2 + owners // 8, owners // 2 + quarter)

    def first_leg(source, relay, send_sem, recv_sem, slot, peer):
        return pltpu.make_async_remote_copy(
            src_ref=source.at[peer],
            dst_ref=relay.at[slot],
            send_sem=send_sem.at[peer],
            recv_sem=recv_sem.at[slot],
            device_id={"pix": behind},
            device_id_type=MESH,
        )

    def second_leg(relay, target, send_sem, recv_sem, slot, offset):
        return pltpu.make_async_remote_copy(
            src_ref=relay.at[slot],
            dst_ref=target.at[ahead],
            send_sem=send_sem.at[slot],
            recv_sem=recv_sem.at[ahead],
            device_id={"pix": flip(ahead, offset, levels)},
            device_id_type=MESH,
        )

    for slot, offset in enumerate(x_relayed):
        first_leg(send_x, relay_x, x_send_sem, x_relay_sem, slot, flip(me, offset, levels)).start()
    for offset in (*range(owners // 2, x_relayed[0]), *range(1, owners // 2), *range(x_relayed[-1] + 1, owners)):
        remote(send_x, got_x, x_send_sem, x_recv_sem, flip(me, offset, levels)).start()
    pltpu.make_async_copy(send_x.at[me], got_x.at[me], x_recv_sem.at[me]).start()

    loads[1].wait()
    loads[2].wait()
    lane = lax.broadcasted_iota(jnp.int32, (TERMS, rows), 1)
    across = harmonic_values(
        days_along(new_dates, dates_count, (TERMS, rows), 1),
        lax.broadcasted_iota(jnp.int32, (TERMS, rows), 0),
    )
    for part_at, part in enumerate(three_parts(across)):
        blocks = [
            jnp.where((lane >= band * dates_count) & (lane < (band + 1) * dates_count), part, 0.0)
            for band in range(bands)
        ]
        right_table[part_at * width:(part_at + 1) * width] = jnp.concatenate(blocks, axis=0).astype(jnp.bfloat16)
    enter_table[...] = fit_table(new_dates, dates_count, bands)
    leave_table[...] = fit_table(old_dates, dates_count, bands)

    for slot, offset in enumerate(x_relayed):
        arrive(relay_x, x_relay_sem, slot)
        second_leg(relay_x, got_x, x_pass_sem, x_recv_sem, slot, offset).start()

    design_rows = across[:, :dates_count]
    paired = jnp.concatenate([design_rows[at:at + 1] * design_rows for at in range(TERMS)], axis=0)
    loads[3].wait()
    loads[4].wait()
    weights = mask_ref[...].astype(jnp.float32).astype(jnp.bfloat16)
    normal = gram_ref[...]
    for part in reversed(three_parts(paired)):
        normal = normal + dot(part.astype(jnp.bfloat16), weights)
    sub = lax.broadcasted_iota(jnp.int32, (TERMS, local_pix), 0)
    matrix = [
        normal[at * TERMS:(at + 1) * TERMS] + jnp.where(sub == at, RIDGE, 0.0) for at in range(TERMS)
    ]
    for pivot in range(TERMS):
        scale = 1.0 / matrix[pivot][pivot:pivot + 1]
        pivot_row = jnp.where(sub == pivot, 1.0, matrix[pivot]) * scale
        for at in range(TERMS):
            if at != pivot:
                matrix[at] = (
                    jnp.where(sub == pivot, 0.0, matrix[at]) - matrix[at][pivot:pivot + 1] * pivot_row
                )
        matrix[pivot] = pivot_row
    for at in range(TERMS):
        inverse_ref[at] = matrix[at]

    square_ref[...] = jnp.zeros_like(square_ref)
    loads[5].wait()

    early = quarter // 2
    late = [*range(x_relayed[0] // 2, x_relayed[-1] // 2 + 1)]
    direct = [at for at in range(quarter, quarter + early) if at not in late]
    order = [*range(early), *direct, *range(early, quarter), *range(quarter + early, tiles), *late]
    order_code = sum(at * tiles**spot for spot, at in enumerate(order))

    def tile_of(code):
        return flip(me // 2, code % tiles, levels - 1)

    def own_step(step, code):
        tile = tile_of(code)
        columns = pl.ds(pl.multiple_of(tile * LANES, LANES), LANES)
        arrive(got_x, x_recv_sem, 2 * tile)
        arrive(got_x, x_recv_sem, 2 * tile + 1)
        low, high = pair_split(
            got_x[2 * tile].astype(jnp.float32), got_x[2 * tile + 1].astype(jnp.float32), half
        )
        entering = jnp.concatenate([low, high], axis=0)
        valid = mask_ref[:, columns].astype(jnp.float32)
        valid = jnp.concatenate([valid] * bands, axis=0)
        parts = dot(right_table[...], (entering * valid).astype(jnp.bfloat16))
        right = (parts[2 * width:] + parts[width:2 * width]) + parts[:width] + rhs_ref[:, columns]
        columns_of = [inverse_ref[at, :, columns] for at in range(TERMS)]
        solved = []
        for band in range(bands):
            total = None
            for at in range(TERMS):
                spot = band * TERMS + at
                term = columns_of[at] * right[spot:spot + 1]
                total = term if total is None else total + term
            solved.append(total)
        coefs = jnp.concatenate(solved, axis=0)
        coef_out[:, columns] = coefs
        low, high = pair_split(coefs[:width // 2], coefs[width // 2:], half)
        send_c[2 * tile] = low
        send_c[2 * tile + 1] = high
        fitted = dot(enter_table[...], stacked_parts(coefs))
        misfit = valid * (entering - fitted)
        square_ref[...] += misfit * misfit

        @pl.when(step > 0)
        def _():
            remote(send_c, got_c, c_send_sem, c_recv_sem, 2 * tile).start()
            remote(send_c, got_c, c_send_sem, c_recv_sem, 2 * tile + 1).start()

        @pl.when(step == 0)
        def _():
            remote(send_c, got_c, c_send_sem, c_recv_sem, flip(me, 1, levels)).start()
            pltpu.make_async_copy(send_c.at[me], got_c.at[me], c_recv_sem.at[me]).start()

        return code // tiles

    lax.fori_loop(0, tiles, own_step, order_code)

    spot = lax.broadcasted_iota(jnp.int32, (1, LANES), 1)
    local = jnp.zeros((1, LANES), jnp.float32)
    for band in range(bands):
        total = jnp.sum(square_ref[band * dates_count:(band + 1) * dates_count], axis=0, keepdims=True)
        local = jnp.where(spot == band, jnp.sum(total, axis=1, keepdims=True), local)
    send_s[...] = local

    def spread_copy(peer):
        return pltpu.make_async_remote_copy(
            src_ref=send_s,
            dst_ref=got_s.at[me],
            send_sem=s_send_sem.at[peer],
            recv_sem=s_recv_sem.at[me],
            device_id={"pix": peer},
            device_id_type=MESH,
        )

    for offset in reversed(range(1, owners)):
        spread_copy(flip(me, offset, levels)).start()
    pltpu.make_async_copy(send_s, got_s.at[me], s_recv_sem.at[me]).start()
    loads[6].wait()

    def rest_step(step, code):
        tile = tile_of(code)
        columns = pl.ds(pl.multiple_of(tile * LANES, LANES), LANES)
        arrive(got_c, c_recv_sem, 2 * tile)
        arrive(got_c, c_recv_sem, 2 * tile + 1)
        low, high = pair_split(got_c[2 * tile], got_c[2 * tile + 1], half)
        fitted = dot(leave_table[...], stacked_parts(jnp.concatenate([low, high], axis=0)))
        rest_ref[:, columns] = old_ref[:, columns].astype(jnp.float32) - fitted
        return code // tiles

    lax.fori_loop(0, tiles, rest_step, order_code)

    for peer in range(owners):
        arrive(got_s, s_recv_sem, peer)
    spread = jnp.sum(got_s[...], axis=0) / (dates_count * local_pix * owners)
    inverse_spread = 1.0 / jnp.sqrt(spread + EPSILON)
    for band in range(bands):
        scale = jnp.sum(jnp.where(spot == band, inverse_spread, 0.0), axis=1, keepdims=True)
        band_rows = slice(band * dates_count, (band + 1) * dates_count)
        rest_ref[band_rows] = rest_ref[band_rows] * scale
    retired_out[...] = rest_ref[...].astype(jnp.bfloat16)

    for offset in range(1, owners):
        peer = flip(me, offset, levels)
        remote(send_x, got_x, x_send_sem, x_recv_sem, peer).wait_send()
        remote(send_c, got_c, c_send_sem, c_recv_sem, peer).wait_send()
        spread_copy(peer).wait_send()
    for slot, offset in enumerate(x_relayed):
        second_leg(relay_x, got_x, x_pass_sem, x_recv_sem, slot, offset).wait_send()


def fused_on_device(new_obs, old_obs, new_mask, new_dates, old_dates, kept_gram, kept_rhs):
    owners = lax.axis_size("pix")
    dates_count, bands, local_pix = new_obs.shape
    rows = dates_count * bands
    width = TERMS * bands
    stay = lambda values: pltpu.with_memory_space_constraint(values, pltpu.HBM)
    band_major = lambda values: stay(values.transpose(1, 0, 2).reshape(-1, local_pix))
    hbm = pl.BlockSpec(memory_space=pltpu.HBM)
    vmem = pl.BlockSpec(memory_space=pltpu.VMEM)
    f32, bf16 = jnp.float32, jnp.bfloat16
    dma = pltpu.SemaphoreType.DMA
    coefs, retired = pl.pallas_call(
        functools.partial(refit_kernel, owners, dates_count, bands, local_pix),
        out_shape=(
            jax.ShapeDtypeStruct((width, local_pix), f32),
            jax.ShapeDtypeStruct((rows, local_pix), bf16),
        ),
        in_specs=[hbm] * 7,
        out_specs=(vmem, vmem),
        scratch_shapes=[
            pltpu.VMEM((rows, local_pix), bf16),
            pltpu.VMEM((rows, local_pix), bf16),
            pltpu.VMEM((dates_count, local_pix), jnp.int32),
            pltpu.VMEM((TERMS * TERMS, local_pix), f32),
            pltpu.VMEM((width, local_pix), f32),
            pltpu.SMEM((dates_count,), jnp.int32),
            pltpu.SMEM((dates_count,), jnp.int32),
            pltpu.VMEM((owners, rows // 2, LANES), bf16),
            pltpu.VMEM((owners, rows // 2, LANES), bf16),
            pltpu.VMEM((owners, width // 2, LANES), f32),
            pltpu.VMEM((owners, width // 2, LANES), f32),
            pltpu.VMEM((1, LANES), f32),
            pltpu.VMEM((owners, 1, LANES), f32),
            pltpu.VMEM((TERMS, TERMS, local_pix), f32),
            pltpu.VMEM((3 * width, rows), bf16),
            pltpu.VMEM((rows, 3 * width), bf16),
            pltpu.VMEM((rows, 3 * width), bf16),
            pltpu.VMEM((rows, LANES), f32),
            pltpu.VMEM((rows, local_pix), f32),
            dma((7,)),
            dma((owners,)), dma((owners,)),
            dma((owners,)), dma((owners,)),
            dma((owners,)), dma((owners,)),
            pltpu.VMEM((owners // 8, rows // 2, LANES), bf16),
            dma((owners // 8,)), dma((owners // 8,)),
        ],
        compiler_params=pltpu.CompilerParams(
            collective_id=0, has_side_effects=True, vmem_limit_bytes=20 << 20
        ),
    )(
        band_major(new_obs), band_major(old_obs), stay(new_mask), stay(new_dates), stay(old_dates),
        stay(kept_gram), band_major(kept_rhs),
    )
    return (
        coefs.reshape(bands, TERMS, local_pix).transpose(1, 0, 2),
        retired.reshape(bands, dates_count, local_pix).transpose(1, 0, 2),
    )


def on_device(*arrays):
    owners = lax.axis_size("pix")
    dates_count, bands, local_pix = arrays[0].shape
    fits = (
        local_pix == owners * (LANES // 2)
        and 16 <= 2 * owners <= 32
        and owners & (owners - 1) == 0
        and arrays[6].shape[0] == TERMS
        and dates_count % 8 == 0
        and bands % 2 == 0
    )
    return fused_on_device(*arrays) if fits else plain_on_device(*arrays)


def solution(mesh):
    return jax.shard_map(
        on_device,
        mesh=mesh,
        in_specs=(
            P(None, None, ("groups", "pix")),
            P(None, None, ("groups", "pix")),
            P(None, ("groups", "pix")),
            P(),
            P(),
            P(None, ("groups", "pix")),
            P(None, None, ("groups", "pix")),
        ),
        out_specs=(P(None, None, ("groups", "pix")), P(None, None, ("groups", "pix"))),
        check_vma=False,
    )
```
